256 devices in a mesh: frame: 32 (over x, z_hi, core), space: 8 (over z_lo, y).
Axes of the slice: x: 4, y: 4, z: 8 (z_hi: 4, z_lo: 2; z = z_hi * 2 + z_lo), core: 2. Of those that a mesh axis runs over, the one named last changes fastest.
Arguments:
- queries: bfloat16 [5120, 3072], P('frame', 'space'), may hold values from -24 to 24
- keys: bfloat16 [5120, 3072], P('frame', 'space'), may hold values from -24 to 24
- values: bfloat16 [5120, 3072], P('frame', 'space'), may hold values from -6 to 6
- grad_out: bfloat16 [5120, 3072], P('frame', 'space'), may hold values from -24 to 24
- proj_weight: bfloat16 [3072, 3072], P('space', 'frame'), may hold values from -0.109375 to 0.109375
Outputs:
- grad_queries: bfloat16 [5120, 3072], P('frame', 'space')
- grad_keys: bfloat16 [5120, 3072], P('frame', 'space')
- grad_values: bfloat16 [5120, 3072], P('frame', 'space')
- grad_proj: float32 [3072, 3072], P('space', 'frame')
The draws below stay inside these ranges and needn't reach their ends.
All inputs are finite; a program needn't handle non-finite values.
Results may differ from the reference program's by a relative error of at most 0.03.
Values may be sent and summed in bfloat16 or wider, within the bound.
A program may use at most 64 MiB of HBM per device.

```python
import jax
import jax.numpy as jnp
from jax import lax

D = 3072
H = 24
HD = 128
L = 5120
N_FRAME = 32


def query_key_pair(key):
    key_q, key_k = jax.random.split(jax.random.fold_in(key, 7177), 2)
    shape = (L, H * HD)
    query_draw = 1.5 * jax.random.truncated_normal(key_q, -6.0, 6.0, shape, jnp.float32)
    key_draw = 1.5 * jax.random.truncated_normal(key_k, -6.0, 6.0, shape, jnp.float32)
    return (query_draw, key_draw)


def draw_queries(key, part):
    return query_key_pair(key)[0].astype(jnp.bfloat16)


def draw_keys(key, part):
    return query_key_pair(key)[1].astype(jnp.bfloat16)


def level_of(stream_key, dims, cuts, low, top_value):
    factor_of = 1.0
    for position, shards_of in cuts:
        heights = jax.random.uniform(jax.random.fold_in(jax.random.fold_in(stream_key, 6), position), (shards_of,), jnp.float32, low / len(cuts), top_value / len(cuts))
        factor_of = factor_of * jnp.repeat(jnp.exp(heights), dims[position] // shards_of).reshape((-1,) + (1,) * (len(dims) - 1 - position))
    return factor_of


def centred(own_key, dims, deviation, reach, cuts=(), held_as=jnp.bfloat16):
    result = jax.random.normal(own_key, dims, jnp.float32) * deviation
    if len(cuts) > 0:
        result = level_of(own_key, dims, cuts, -0.22, 0.18) * result
    return jnp.clip(result, min=-reach, max=reach).astype(held_as)


def setup_inputs(seed: int = 0) -> dict:
    seeds = jax.random.split(jax.random.key(seed), 6)
    queries = draw_queries(jax.random.fold_in(seeds[5], 71), 0)
    keys = draw_keys(jax.random.fold_in(seeds[5], 71), 0)
    values = centred(seeds[2], (L, H * HD), 1.0, 6.0, ((0, 32), (1, 8)))
    grad_out = centred(seeds[3], (L, D), 4.0, 24.0, ((0, 32), (1, 8)))
    proj_weight = centred(seeds[4], (H * HD, D), (H * HD) ** -0.5, 0.109375, ((0, 8), (1, 32)))
    return {"queries": queries, "keys": keys, "values": values, "grad_out": grad_out, "proj_weight": proj_weight}


def head_grads(inputs):
    query_h, key_h, value_h, grad_h = inputs
    factor = 1.0 / jnp.sqrt(jnp.float32(HD))
    seq_len = query_h.shape[0]
    group_rows = seq_len // N_FRAME
    logits = jnp.dot(query_h, key_h.T, preferred_element_type=jnp.float32) * factor
    row_max = lax.optimization_barrier(jnp.max(logits, axis=1, keepdims=True))
    log_norm = row_max + jnp.log(lax.optimization_barrier(jnp.sum(jnp.exp(logits - row_max), axis=1, keepdims=True)))
    probs = jnp.exp(logits - log_norm)
    probs_low = probs.astype(jnp.bfloat16)
    attn_out = jnp.dot(probs_low, value_h, preferred_element_type=jnp.float32).astype(jnp.bfloat16)
    row_delta = lax.optimization_barrier(jnp.sum(grad_h.astype(jnp.float32) * attn_out.astype(jnp.float32), axis=1, keepdims=True))
    grad_probs = jnp.dot(grad_h, value_h.T, preferred_element_type=jnp.float32)
    grad_logits = (probs * (grad_probs - row_delta)).astype(jnp.bfloat16)
    grad_query = (factor * jnp.dot(grad_logits, key_h, preferred_element_type=jnp.float32)).astype(jnp.bfloat16)
    grouped_logits = grad_logits.reshape(N_FRAME, group_rows, seq_len).astype(jnp.float32)
    grouped_probs = probs_low.reshape(N_FRAME, group_rows, seq_len).astype(jnp.float32)
    grouped_query = query_h.reshape(N_FRAME, group_rows, HD).astype(jnp.float32)
    grouped_grad = grad_h.reshape(N_FRAME, group_rows, HD).astype(jnp.float32)
    key_part = (factor * jnp.einsum('gqk,gqd->gkd', grouped_logits, grouped_query)).astype(jnp.bfloat16)
    value_part = jnp.einsum('gqk,gqd->gkd', grouped_probs, grouped_grad).astype(jnp.bfloat16)
    key_part = lax.optimization_barrier(key_part)
    value_part = lax.optimization_barrier(value_part)
    grad_key = lax.optimization_barrier(jnp.sum(key_part.astype(jnp.float32), axis=0)).astype(jnp.bfloat16)
    grad_value = lax.optimization_barrier(jnp.sum(value_part.astype(jnp.float32), axis=0)).astype(jnp.bfloat16)
    return (attn_out, grad_query, grad_key, grad_value)

def by_heads(matrix):
    return matrix.reshape(matrix.shape[0], H, HD).transpose(1, 0, 2)

def to_rows(stacked):
    return stacked.transpose(1, 0, 2).reshape(stacked.shape[1], H * HD)

def reference(queries, keys, values, grad_out, proj_weight):
    grad_attn = jnp.dot(grad_out, proj_weight.T, preferred_element_type=jnp.float32).astype(jnp.bfloat16)
    attn_out, grad_query, grad_key, grad_value = lax.map(head_grads, (by_heads(queries), by_heads(keys), by_heads(values), by_heads(grad_attn)))
    attn_rows = to_rows(attn_out)
    grad_proj = jnp.dot(attn_rows.T, grad_out, preferred_element_type=jnp.float32)
    return (to_rows(grad_query), to_rows(grad_key), to_rows(grad_value), grad_proj)
```

```python
import math

import jax
import jax.numpy as jnp
from jax import lax
from jax.experimental import pallas as pl
from jax.experimental.pallas import tpu as pltpu
from jax.sharding import PartitionSpec as P

HD = 128
MESH = pl.DeviceIdType.MESH
F32 = jnp.float32
BF16 = jnp.bfloat16
RING = 4
CORES = 2
PAIR = 2


def mm(a, b):
    return jnp.dot(a, b, preferred_element_type=F32)


def kernel(dims, q_ref, k_ref, v_ref, g_ref, w_ref, dq_ref, dk_ref, dv_ref, gp_ref, *scratch):
    rows, heads, wcols, nsem = dims
    (q4, k8, v8, g8, wb, da, do4, qt, kt, vt, dot_, don, s_buf, p_buf, ot, st_out, st_in,
     ob, ol, dqt, dqb, dql, dkb, dvb, dkc, dvc, dkl, dvl, gpb, gpc, gpx, gpz, gpr,
     send_sems, recv_sems) = scratch
    width = heads * HD
    nq = RING * rows
    kc = CORES * rows
    factor = 1.0 / math.sqrt(HD)
    c2 = factor * math.log2(math.e)

    f = lax.axis_index("frame")
    s = lax.axis_index("space")
    x, zh, core = f // 8, lax.rem(f // 2, 4), lax.rem(f, 2)
    zl, y = s // 4, lax.rem(s, 4)

    def around(i, k):
        return lax.rem(i + k, RING)

    def dev_f(xx, zz, cc):
        return {"frame": (xx * RING + zz) * CORES + cc}

    xs = [dev_f(around(x, k), zh, core) for k in range(4)]
    zs = [dev_f(x, around(zh, k), core) for k in range(4)]
    sib = dev_f(x, zh, 1 - core)
    ys = [{"space": zl * RING + around(y, k)} for k in range(4)]
    zsib = {"space": (1 - zl) * RING + y}

    partners = [zs[1], zs[2], zs[3], xs[1], xs[3], ys[1], ys[3], sib, zsib]
    barrier = pltpu.get_barrier_semaphore()
    for other in partners:
        pl.semaphore_signal(barrier, inc=1, device_id=other, device_id_type=MESH)
    pl.semaphore_wait(barrier, len(partners))

    used = [0]
    pending = []

    def send(src, dst, device):
        n = used[0]
        used[0] += 1
        copy = pltpu.make_async_remote_copy(
            src_ref=src, dst_ref=dst, send_sem=send_sems.at[n], recv_sem=recv_sems.at[n],
            device_id=device, device_id_type=MESH)
        copy.start()
        pending.append(copy)
        return copy

    def gather(own, at, lo, hi, i, devs, forward=None):
        p, n, o = around(i, 1), around(i, 3), around(i, 2)
        c0 = send(own, at(i), devs[1])
        c1 = send(own, at(i), devs[3])
        fw = []
        if forward is not None:
            fw.append(send(own, at(i), forward))
        yield
        c0.wait_recv()
        c2 = send(lo(n), lo(n), devs[1])
        if forward is not None:
            fw.append(send(at(n), at(n), forward))
        c1.wait_recv()
        c3 = send(hi(p), hi(p), devs[3])
        if forward is not None:
            fw.append(send(at(p), at(p), forward))
        yield
        c2.wait_recv()
        c3.wait_recv()
        if forward is not None:
            fw.append(send(at(o), at(o), forward))
            yield
            for c in fw:
                c.wait_recv()

    def add_into(dst, landed):
        dst[...] = (dst[...].astype(F32) + landed[...].astype(F32)).astype(BF16)

    def scatter(blk, size, land, i, devs, out):
        h = size // 2
        p, n, o = around(i, 1), around(i, 3), around(i, 2)
        a0, b0 = land.at[0, 0:h], land.at[0, h:size]
        from_n, from_p = land.at[1], land.at[2]
        c0 = send(blk(o, 0, h), a0, devs[1])
        c1 = send(blk(o, h, size), b0, devs[3])
        c2 = send(blk(p, h, size), land.at[1, h:size], devs[1])
        c3 = send(blk(n, 0, h), land.at[2, 0:h], devs[3])
        yield
        c0.wait_recv()
        add_into(blk(p, 0, h), a0)
        c4 = send(blk(p, 0, h), land.at[1, 0:h], devs[1])
        c1.wait_recv()
        add_into(blk(n, h, size), b0)
        c5 = send(blk(n, h, size), land.at[2, h:size], devs[3])
        yield
        for c in (c2, c3, c4, c5):
            c.wait_recv()
        out(blk(i, 0, size)[...].astype(F32) + from_n[...].astype(F32) + from_p[...].astype(F32))

    def pump(*flows):
        for flow in flows:
            next(flow, None)

    half = rows // 2
    wz = gather(w_ref, lambda j: wb.at[x, j, core], lambda j: wb.at[x, j, core, 0:wcols // 2],
                lambda j: wb.at[x, j, core, wcols // 2:wcols], zh, zs)
    qz = gather(q_ref, lambda j: q4.at[j], lambda j: q4.at[j, 0:half],
                lambda j: q4.at[j, half:rows], zh, zs)
    kx = gather(k_ref, lambda j: k8.at[j, core], lambda j: k8.at[j, core, 0:half],
                lambda j: k8.at[j, core, half:rows], x, xs, sib)
    vx = gather(v_ref, lambda j: v8.at[j, core], lambda j: v8.at[j, core, 0:half],
                lambda j: v8.at[j, core, half:rows], x, xs, sib)
    pump(wz)
    gz = send(g_ref, g8.at[zl, y], zsib)
    pump(kx, qz, vx)
    g8[zl, y] = g_ref[...]
    wb[x, zh, core] = w_ref[...]
    q4[zh] = q_ref[...]
    k8[x, core] = k_ref[...]
    v8[x, core] = v_ref[...]

    gz.wait_recv()
    gy = gather(g8.at[:, y], lambda j: g8.at[:, j], lambda j: g8.at[0, j],
                lambda j: g8.at[1, j], y, ys)
    pump(gy)
    pump(wz, kx, qz)
    pump(wz)
    wx = gather(wb.at[x, :, core], lambda j: wb.at[j, :, core], lambda j: wb.at[j, 0:2, core],
                lambda j: wb.at[j, 2:4, core], x, xs, sib)
    pump(wx)
    pump(vx, gy, kx, qz, kx)

    def cols(h):
        return slice(h * HD, (h + 1) * HD)

    for h in range(heads):
        qt[h] = q4[:, :, cols(h)].reshape(nq, HD).T
    for h in range(heads):
        for j in range(RING):
            kt[h, j] = k8[j, :, :, cols(h)].reshape(kc, HD).T

    st_out[...] = jnp.zeros_like(st_out)

    def logits_pass(h):
        def body(j, m8):
            sc = mm(k8[j, :, :, cols(h)].reshape(kc, HD), qt[h])
            s_buf[j] = sc
            return jnp.maximum(m8, jnp.max(sc.reshape(kc // 8, 8, nq), axis=0))
        m8 = lax.fori_loop(0, RING, body, jnp.full((8, nq), -jnp.inf, F32))
        return jnp.max(m8, axis=0, keepdims=True)

    def probs_pass(h, m):
        ot[h] = jnp.zeros((HD, nq), F32)

        def body(j, l8):
            pr = jnp.exp2((s_buf[j] - m) * c2)
            low = pr.astype(BF16)
            p_buf[h, j] = low
            ot[h] += mm(vt[h, j], low)
            return l8 + jnp.sum(pr.reshape(kc // 8, 8, nq), axis=0)
        l8 = lax.fori_loop(0, RING, body, jnp.zeros((8, nq), F32))
        st_out[h:h + 1] = m
        st_out[8 + h:9 + h] = jnp.sum(l8, axis=0, keepdims=True)

    m = logits_pass(0)
    pump(wx, vx, vx)
    for h in range(heads):
        for j in range(RING):
            vt[h, j] = v8[j, :, :, cols(h)].reshape(kc, HD).T
    probs_pass(0, m)
    pump(wx, gy)
    for h in range(1, heads - 1):
        probs_pass(h, logits_pass(h))
    pump(wx)

    acc = jnp.zeros((rows, width), F32)
    for t in range(PAIR * RING):
        block = wb[t // 2, 2 * (t % 2):2 * (t % 2) + 2].reshape(width, width)
        acc = acc + mm(g8[t // RING, t % RING], block)
    da[...] = acc.astype(BF16)
    dz = gather(da, lambda j: do4.at[j], lambda j: do4.at[j, 0:half],
                lambda j: do4.at[j, half:rows], zh, zs)
    pump(dz)
    do4[zh] = da[...]
    m = logits_pass(heads - 1)
    pump(dz)
    probs_pass(heads - 1, m)
    pump(dz)

    for h in range(heads):
        dt = do4[:, :, cols(h)].reshape(nq, HD).astype(F32).T
        dot_[h] = dt
        st_out[16 + h:17 + h] = jnp.sum(dt * ot[h], axis=0, keepdims=True)

    st = [send(st_out, st_in.at[zh], zs[k]) for k in (1, 2, 3)]
    for c in st:
        c.wait_recv()
    st_in[zh] = st_out[...]
    ms = [st_in[j, 0:8] for j in range(RING)]
    m_all = jnp.maximum(jnp.maximum(ms[0], ms[1]), jnp.maximum(ms[2], ms[3]))
    es = [jnp.exp2((mj - m_all) * c2) for mj in ms]
    l_all = sum(es[j] * st_in[j, 8:16] for j in range(RING))
    u_all = sum(es[j] * st_in[j, 16:24] for j in range(RING))
    inv = 1.0 / jnp.where(l_all > 0.0, l_all, 1.0)
    scale = jnp.exp2((st_out[0:8] - m_all) * c2) * inv
    delta = u_all * inv * scale

    for h in range(heads):
        o_n = (ot[h] * scale[h:h + 1]).T
        ob[:, :, cols(h)] = o_n.astype(BF16).reshape(RING, rows, HD)
    attn = {}

    def keep_attn(value):
        attn["out"] = value.astype(BF16)

    oz = scatter(lambda j, lo, hi: ob.at[j, lo:hi], rows, ol, zh, zs, keep_attn)
    pump(oz)

    def backward(h):
        ds_h = dot_[h] * scale[h:h + 1]
        dsl = ds_h.astype(BF16)
        don[...] = ds_h.T.astype(BF16)
        dl = delta[h:h + 1]
        dqt[...] = jnp.zeros_like(dqt)

        def body(j, unused):
            dp = mm(v8[j, :, :, cols(h)].reshape(kc, HD), dsl)
            pr = p_buf[h, j]
            dlog = (pr.astype(F32) * (dp - dl)).astype(BF16)
            dvb[h, :, j] = mm(pr, don[...]).astype(BF16).reshape(CORES, rows, HD)
            dkb[h, :, j] = (factor * mm(dlog, q4[:, :, cols(h)].reshape(nq, HD))).astype(
                BF16).reshape(CORES, rows, HD)
            dqt[...] += mm(kt[h, j], dlog)
            return unused
        lax.fori_loop(0, RING, body, 0)
        dqb[h] = (factor * dqt[...]).T.astype(BF16).reshape(RING, rows, HD)

    def pair_then_ring(part, landc, land, h, out):
        c = send(part.at[h, 1 - core], landc.at[h], sib)
        yield
        c.wait_recv()
        mine = part.at[h, core]
        add_into(mine, landc.at[h])
        ring = scatter(lambda j, lo, hi: part.at[h, core, j, lo:hi], rows, land.at[h], x, xs, out)
        yield from ring

    def writer(ref, h):
        def write(value):
            ref[:, cols(h)] = value.astype(BF16)
        return write

    flows = []

    def exits(h):
        return [pair_then_ring(dkb, dkc, dkl, h, writer(dk_ref, h)),
                pair_then_ring(dvb, dvc, dvl, h, writer(dv_ref, h)),
                scatter(lambda j, lo, hi: dqb.at[h, j, lo:hi], rows, dql.at[h], zh, zs,
                        writer(dq_ref, h))]

    backward(0)
    flows.append(exits(0))
    pump(*flows[0])
    pump(oz, *flows[0][:2])
    backward(1)
    flows.append(exits(1))
    pump(*flows[1])
    pump(oz, *flows[0])
    pump(*flows[1][:2])

    out_low = attn["out"]
    for t in range(PAIR * RING):
        part = lax.dot_general(g8[t // RING, t % RING], out_low, (((0,), (0,)), ((), ())),
                               preferred_element_type=F32)
        gpb[t // 2, 2 * (t % 2):2 * (t % 2) + 2] = part.astype(BF16).reshape(
            2, CORES, wcols, width)

    def proj_flow():
        c = send(gpb.at[:, :, 1 - core], gpc, sib)
        yield
        c.wait_recv()
        for j in range(RING):
            add_into(gpb.at[j, :, core], gpc.at[j])

        def keep(value):
            gpr[...] = value.astype(BF16)
        yield from scatter(lambda j, lo, hi: gpb.at[j, lo:hi, core], RING, gpx, x, xs, keep)

        def final(value):
            gp_ref[...] = value
        yield from scatter(lambda j, lo, hi: gpr.at[j, lo:hi], wcols, gpz, zh, zs, final)

    gpf = proj_flow()
    pump(gpf)
    backward(2)
    flows.append(exits(2))
    pump(gpf)
    pump(*flows[2])
    for fl in flows[0]:
        pump(fl)
    for fl in flows[1]:
        pump(fl)
    pump(gpf)
    live = flows[2] + flows[1] + flows[0] + [gpf]
    while live:
        live = [fl for fl in live if next(fl, True) is None]
    for c in pending:
        c.wait_send()
    assert used[0] <= nsem, used[0]


def local(queries, keys, values, grad_out, proj_weight):
    rows, width = queries.shape
    heads = width // HD
    wcols = proj_weight.shape[1]
    nq, kc = RING * rows, CORES * rows
    nsem = 144

    def vm(*shape, dtype=BF16):
        return pltpu.VMEM(shape, dtype)

    scratch = [
        vm(RING, rows, width), vm(RING, CORES, rows, width), vm(RING, CORES, rows, width),
        vm(PAIR, RING, rows, width), vm(RING, RING, CORES, wcols, width),
        vm(rows, width), vm(RING, rows, width),
        vm(heads, HD, nq), vm(heads, RING, HD, kc), vm(heads, RING, HD, kc),
        vm(heads, HD, nq, dtype=F32), vm(nq, HD),
        vm(RING, kc, nq, dtype=F32), vm(heads, RING, kc, nq), vm(heads, HD, nq, dtype=F32),
        vm(24, nq, dtype=F32), vm(RING, 24, nq, dtype=F32),
        vm(RING, rows, width), vm(3, rows, width),
        vm(HD, nq, dtype=F32), vm(heads, RING, rows, HD), vm(heads, 3, rows, HD),
        vm(heads, CORES, RING, rows, HD), vm(heads, CORES, RING, rows, HD),
        vm(heads, RING, rows, HD), vm(heads, RING, rows, HD),
        vm(heads, 3, rows, HD), vm(heads, 3, rows, HD),
        vm(RING, RING, CORES, wcols, width), vm(RING, RING, wcols, width),
        vm(3, RING, wcols, width), vm(3, wcols, width), vm(RING, wcols, width),
        pltpu.SemaphoreType.DMA((nsem,)), pltpu.SemaphoreType.DMA((nsem,)),
    ]
    vmem = pl.BlockSpec(memory_space=pltpu.VMEM)

    def body(*refs):
        kernel((rows, heads, wcols, nsem), *refs)

    like = jax.ShapeDtypeStruct((rows, width), BF16)
    dq, dk, dv, gp = pl.pallas_call(
        body,
        out_shape=(like, like, like, jax.ShapeDtypeStruct((wcols, width), F32)),
        in_specs=[vmem] * 5,
        out_specs=(vmem,) * 4,
        scratch_shapes=scratch,
        compiler_params=pltpu.CompilerParams(
            collective_id=0, has_side_effects=True, vmem_limit_bytes=60 * 1024 * 1024),
        name="fused",
    )(queries, keys, values, grad_out, proj_weight.T)
    return dq, dk, dv, gp.T


def solution(mesh):
    spec = P("frame", "space")
    return jax.shard_map(
        local, mesh=mesh, in_specs=(spec,) * 4 + (P("space", "frame"),),
        out_specs=(spec,) * 3 + (P("space", "frame"),), check_vma=False)
```

```python
import math

import jax
import jax.numpy as jnp
from jax import lax
from jax.experimental import pallas as pl
from jax.experimental.pallas import tpu as pltpu
from jax.sharding import PartitionSpec as P

HD = 128
MESH = pl.DeviceIdType.MESH
F32 = jnp.float32
BF16 = jnp.bfloat16
RING = 4
CORES = 2
PAIR = 2


def mm(a, b):
    return jnp.dot(a, b, preferred_element_type=F32)


def kernel(dims, q_ref, k_ref, v_ref, g_ref, w_ref, dq_ref, dk_ref, dv_ref, gp_ref, *scratch):
    rows, heads, wcols, nsem = dims
    (q4, kv8, g8, gt, wb, da, do4, qt, kt, vt, don, s_buf, p_buf, ot, l_in, u_out, l_out, u_in,
     ob, ol, dqt, dqb, dql, dkvb, dkvc, dkvl, gpb, gpc, gpx, gpz, gpr,
     send_sems, recv_sems) = scratch
    width = heads * HD
    nq = RING * rows
    kc = CORES * rows
    factor = 1.0 / math.sqrt(HD)
    c2 = factor * math.log2(math.e)

    f = lax.axis_index("frame")
    s = lax.axis_index("space")
    x, zh, core = f // 8, lax.rem(f // 2, 4), lax.rem(f, 2)
    zl, y = s // 4, lax.rem(s, 4)

    def around(i, k):
        return lax.rem(i + k, RING)

    def dev_f(xx, zz, cc):
        return {"frame": (xx * RING + zz) * CORES + cc}

    xs = [dev_f(around(x, k), zh, core) for k in range(4)]
    zs = [dev_f(x, around(zh, k), core) for k in range(4)]
    sib = dev_f(x, zh, 1 - core)
    ys = [{"space": zl * RING + around(y, k)} for k in range(4)]
    zsib = {"space": (1 - zl) * RING + y}

    partners = [zs[1], zs[3], xs[1], xs[3], ys[1], ys[3], sib, zsib]
    barrier = pltpu.get_barrier_semaphore()
    for other in partners:
        pl.semaphore_signal(barrier, inc=1, device_id=other, device_id_type=MESH)
    pl.semaphore_wait(barrier, len(partners))

    used = [0]
    pending = []

    def send(src, dst, device):
        n = used[0]
        used[0] += 1
        copy = pltpu.make_async_remote_copy(
            src_ref=src, dst_ref=dst, send_sem=send_sems.at[n], recv_sem=recv_sems.at[n],
            device_id=device, device_id_type=MESH)
        copy.start()
        pending.append(copy)
        return copy

    def gather(own, at, lo, hi, i, devs, forward=None):
        p, n, o = around(i, 1), around(i, 3), around(i, 2)
        first = [(send(src, dst, devs[1]), send(src, dst, devs[3])) for src, dst in own]
        fw = []
        if forward is not None:
            fw += [send(src, dst, forward) for src, dst in own]
        yield
        for c0, _ in first:
            c0.wait_recv()
        c2 = send(lo(n), lo(n), devs[1])
        if forward is not None:
            fw.append(send(at(n), at(n), forward))
        for _, c1 in first:
            c1.wait_recv()
        c3 = send(hi(p), hi(p), devs[3])
        if forward is not None:
            fw.append(send(at(p), at(p), forward))
        yield
        c2.wait_recv()
        c3.wait_recv()
        if forward is not None:
            fw.append(send(at(o), at(o), forward))
            yield
            for c in fw:
                c.wait_recv()

    def add_into(dst, landed):
        dst[...] = (dst[...].astype(F32) + landed[...].astype(F32)).astype(BF16)

    def scatter(blk, size, land, i, devs, out):
        h = size // 2
        p, n, o = around(i, 1), around(i, 3), around(i, 2)
        a0, b0 = land.at[0, 0:h], land.at[0, h:size]
        from_n, from_p = land.at[1], land.at[2]
        c0 = send(blk(o, 0, h), a0, devs[1])
        c1 = send(blk(o, h, size), b0, devs[3])
        c2 = send(blk(p, h, size), land.at[1, h:size], devs[1])
        c3 = send(blk(n, 0, h), land.at[2, 0:h], devs[3])
        yield
        c0.wait_recv()
        add_into(blk(p, 0, h), a0)
        c4 = send(blk(p, 0, h), land.at[1, 0:h], devs[1])
        c1.wait_recv()
        add_into(blk(n, h, size), b0)
        c5 = send(blk(n, h, size), land.at[2, h:size], devs[3])
        yield
        for c in (c2, c3, c4, c5):
            c.wait_recv()
        out(blk(i, 0, size)[...].astype(F32) + from_n[...].astype(F32) + from_p[...].astype(F32))

    def spread(src, land):
        copies = [send(src, land.at[zh], zs[k]) for k in (1, 3, 2)]
        yield
        for c in copies:
            c.wait_recv()

    def pump(*flows):
        for flow in flows:
            next(flow, None)

    def cols(h):
        return slice(h * HD, (h + 1) * HD)

    half = rows // 2
    hw = wcols // 2
    H = range(heads)

    def q_flow(h):
        own = [(q_ref.at[:, cols(h)], q4.at[h, zh])]
        return gather(own, lambda j: q4.at[h, j], lambda j: q4.at[h, j, 0:half],
                      lambda j: q4.at[h, j, half:rows], zh, zs)

    def kv_flow(h):
        own = [(k_ref.at[:, cols(h)], kv8.at[h, x, core, 0]),
               (v_ref.at[:, cols(h)], kv8.at[h, x, core, 1])]
        return gather(own, lambda j: kv8.at[h, j, core], lambda j: kv8.at[h, j, core, 0],
                      lambda j: kv8.at[h, j, core, 1], x, xs, sib)

    def wz_flow(h):
        own = [(w_ref.at[:, cols(h)], wb.at[h, x, zh, core])]
        return gather(own, lambda j: wb.at[h, x, j, core], lambda j: wb.at[h, x, j, core, 0:hw],
                      lambda j: wb.at[h, x, j, core, hw:wcols], zh, zs)

    def wx_flow(h):
        own = [(wb.at[h, x, :, core], wb.at[h, x, :, core])]
        return gather(own, lambda j: wb.at[h, j, :, core], lambda j: wb.at[h, j, 0:2, core],
                      lambda j: wb.at[h, j, 2:4, core], x, xs, sib)

    def g_flow():
        c = send(g_ref, g8.at[zl, y], zsib)
        yield
        c.wait_recv()
        own = [(g8.at[:, y], g8.at[:, y])]
        yield from gather(own, lambda j: g8.at[:, j], lambda j: g8.at[0, j],
                          lambda j: g8.at[1, j], y, ys)

    def do_flow(h):
        own = [(da.at[h], do4.at[h, zh])]
        return gather(own, lambda j: do4.at[h, j], lambda j: do4.at[h, j, 0:half],
                      lambda j: do4.at[h, j, half:rows], zh, zs)

    def turn(h):
        qt[h] = q4[h].reshape(nq, HD).T
        for j in range(RING):
            kt[h, j] = kv8[h, j, :, 0].reshape(kc, HD).T
            vt[h, j] = kv8[h, j, :, 1].reshape(kc, HD).T

    def logits_pass(h):
        def body(j, m8):
            sc = mm(kv8[h, j, :, 0].reshape(kc, HD), qt[h])
            s_buf[j] = sc
            return jnp.maximum(m8, jnp.max(sc.reshape(kc // 8, 8, nq), axis=0))
        m8 = lax.fori_loop(0, RING, body, jnp.full((8, nq), -jnp.inf, F32))
        return jnp.max(m8, axis=0, keepdims=True)

    def probs_pass(h, m):
        ot[h] = jnp.zeros((HD, nq), F32)

        def body(j, l8):
            pr = jnp.exp2((s_buf[j] - m) * c2)
            low = pr.astype(BF16)
            p_buf[h, j] = low
            ot[h] += mm(vt[h, j], low)
            return l8 + jnp.sum(pr.reshape(kc // 8, 8, nq), axis=0)
        l8 = lax.fori_loop(0, RING, body, jnp.zeros((8, nq), F32))
        l_out[h] = m * c2 + jnp.log2(jnp.sum(l8, axis=0, keepdims=True))

    scales = {}

    def normalise(h, m):
        l_in[h, zh] = l_out[h]
        ls = [l_in[h, j] for j in range(RING)]
        top = jnp.maximum(jnp.maximum(ls[0], ls[1]), jnp.maximum(ls[2], ls[3]))
        total = sum(jnp.exp2(v - top) for v in ls)
        scales[h] = jnp.exp2(m * c2 - (top + jnp.log2(total)))
        ob[h] = (ot[h] * scales[h]).T.astype(BF16).reshape(RING, rows, HD)

    attn = {}

    def o_flow(h):
        def keep(value):
            attn[h] = value.astype(BF16)
        return scatter(lambda j, lo, hi: ob.at[h, j, lo:hi], rows, ol.at[h], zh, zs, keep)

    def grad_attn(h):
        acc = jnp.zeros((rows, HD), F32)
        for t in range(PAIR * RING):
            block = wb[h, t // 2, 2 * (t % 2):2 * (t % 2) + 2].reshape(width, HD)
            acc = acc + mm(g8[t // RING, t % RING], block)
        low = acc.astype(BF16)
        da[h] = low
        do4[h, zh] = low

    grads = {}

    def row_terms(h):
        scaled = do4[h].reshape(nq, HD).astype(F32).T * scales[h]
        u_out[h] = jnp.sum(scaled * ot[h], axis=0, keepdims=True)
        grads[h] = scaled

    def backward(h):
        u_in[h, zh] = u_out[h]
        dl = (u_in[h, 0] + u_in[h, 1] + u_in[h, 2] + u_in[h, 3]) * scales[h]
        dsl = grads[h].astype(BF16)
        don[...] = grads[h].T.astype(BF16)
        dqt[...] = jnp.zeros_like(dqt)

        def body(j, unused):
            dp = mm(kv8[h, j, :, 1].reshape(kc, HD), dsl)
            pr = p_buf[h, j]
            dlog = (pr.astype(F32) * (dp - dl)).astype(BF16)
            dkvb[h, :, j, 1] = mm(pr, don[...]).astype(BF16).reshape(CORES, rows, HD)
            dkvb[h, :, j, 0] = (factor * mm(dlog, q4[h].reshape(nq, HD))).astype(
                BF16).reshape(CORES, rows, HD)
            dqt[...] += mm(kt[h, j], dlog)
            return unused
        lax.fori_loop(0, RING, body, 0)
        dqb[h] = (factor * dqt[...]).T.astype(BF16).reshape(RING, rows, HD)

    def proj(h):
        for t in range(PAIR * RING):
            part = mm(gt[t], attn[h])
            gpb[h, t // 2, 2 * (t % 2):2 * (t % 2) + 2] = part.astype(BF16).reshape(
                2, CORES, wcols, HD)

    def dkv_flow(h):
        c = send(dkvb.at[h, 1 - core], dkvc.at[h], sib)
        yield
        c.wait_recv()
        add_into(dkvb.at[h, core], dkvc.at[h])

        def write(value):
            dk_ref[:, cols(h)] = value[0].astype(BF16)
            dv_ref[:, cols(h)] = value[1].astype(BF16)
        yield from scatter(lambda j, lo, hi: dkvb.at[h, core, j, lo:hi], 2, dkvl.at[h], x, xs,
                           write)

    def dq_flow(h):
        def write(value):
            dq_ref[:, cols(h)] = value.astype(BF16)
        return scatter(lambda j, lo, hi: dqb.at[h, j, lo:hi], rows, dql.at[h], zh, zs, write)

    def gp_flow(h):
        c = send(gpb.at[h, :, :, 1 - core], gpc.at[h], sib)
        yield
        c.wait_recv()
        for j in range(RING):
            add_into(gpb.at[h, j, :, core], gpc.at[h, j])

        def keep(value):
            gpr[h] = value.astype(BF16)
        yield from scatter(lambda j, lo, hi: gpb.at[h, j, lo:hi, core], RING, gpx.at[h], x, xs,
                           keep)

        def final(value):
            gp_ref[:, cols(h)] = value
        yield from scatter(lambda j, lo, hi: gpr.at[h, j, lo:hi], wcols, gpz.at[h], zh, zs, final)

    QZ, KV, WZ = [q_flow(h) for h in H], [kv_flow(h) for h in H], [wz_flow(h) for h in H]
    WX, DZ, OZ = [wx_flow(h) for h in H], [do_flow(h) for h in H], [o_flow(h) for h in H]
    LX = [spread(l_out.at[h], l_in.at[h]) for h in H]
    UX = [spread(u_out.at[h], u_in.at[h]) for h in H]
    DK, DQ, GP = [dkv_flow(h) for h in H], [dq_flow(h) for h in H], [gp_flow(h) for h in H]
    G = g_flow()

    pump(QZ[0], KV[0], WZ[0], G)
    g8[zl, y] = g_ref[...]
    for h in H:
        q4[h, zh] = q_ref[:, cols(h)]
        kv8[h, x, core, 0] = k_ref[:, cols(h)]
        kv8[h, x, core, 1] = v_ref[:, cols(h)]
        wb[h, x, zh, core] = w_ref[:, cols(h)]
    pump(QZ[0], KV[0], QZ[1], KV[1], WZ[0], WZ[1])
    pump(G, KV[0], QZ[0], WZ[0], WX[0], KV[0], QZ[2], KV[2])
    turn(0)
    m0 = logits_pass(0)
    pump(QZ[1], KV[1], WZ[1], WZ[2])
    probs_pass(0, m0)
    pump(LX[0], G, WX[0], QZ[1], KV[1], WZ[1], WX[1], QZ[2], KV[2], KV[1])
    turn(1)
    m1 = logits_pass(1)
    pump(WX[0])
    probs_pass(1, m1)
    pump(LX[1], WZ[2], QZ[2], KV[2], KV[2], LX[0])
    normalise(0, m0)
    pump(OZ[0], WX[0], G)
    grad_attn(0)
    pump(DZ[0], WZ[2], WX[1], WX[2])
    turn(2)
    m2 = logits_pass(2)
    probs_pass(2, m2)
    pump(LX[2], OZ[0], DZ[0], WX[1], WX[1])
    grad_attn(1)
    pump(DZ[1], LX[1])
    normalise(1, m1)
    pump(OZ[1], WX[2], DZ[0])
    row_terms(0)
    pump(UX[0])
    for t in range(PAIR * RING):
        gt[t] = g8[t // RING, t % RING].T
    pump(OZ[0])
    proj(0)
    pump(GP[0], WX[2], WX[2])
    grad_attn(2)
    pump(DZ[2], LX[2])
    normalise(2, m2)
    pump(OZ[2], DZ[1], OZ[1], UX[0])
    backward(0)
    pump(DK[0], DQ[0], GP[0], DZ[1])
    row_terms(1)
    pump(UX[1], OZ[1])
    proj(1)
    pump(GP[1], DZ[2], OZ[2], GP[0], DK[0], DQ[0], UX[1])
    backward(1)
    pump(DK[1], DQ[1], DZ[2])
    row_terms(2)
    pump(UX[2], OZ[2])
    proj(2)
    pump(GP[2], GP[1], GP[0], DK[0], DQ[0], DK[1], DQ[1], UX[2])
    backward(2)
    pump(DK[2], DQ[2], GP[2], GP[1], GP[0], DK[1], DQ[1], DK[0])
    pump(GP[1], GP[2], DK[2], DQ[2], GP[0])
    pump(GP[2], GP[1], DK[2], DQ[2], DK[1])
    pump(GP[2], GP[1], DK[2])
    pump(GP[2])
    for flow in QZ + KV + WZ + WX + DZ + OZ + LX + UX + DK + DQ + GP + [G]:
        for _ in flow:
            pass
    for c in pending:
        c.wait_send()
    assert used[0] <= nsem, used[0]


def local(queries, keys, values, grad_out, proj_weight):
    rows, width = queries.shape
    heads = width // HD
    wcols = proj_weight.shape[1]
    nq, kc = RING * rows, CORES * rows
    nsem = 240

    def vm(*shape, dtype=BF16):
        return pltpu.VMEM(shape, dtype)

    scratch = [
        vm(heads, RING, rows, HD), vm(heads, RING, CORES, 2, rows, HD),
        vm(PAIR, RING, rows, width), vm(PAIR * RING, width, rows),
        vm(heads, RING, RING, CORES, wcols, HD),
        vm(heads, rows, HD), vm(heads, RING, rows, HD),
        vm(heads, HD, nq), vm(heads, RING, HD, kc), vm(heads, RING, HD, kc),
        vm(nq, HD),
        vm(RING, kc, nq, dtype=F32), vm(heads, RING, kc, nq), vm(heads, HD, nq, dtype=F32),
        vm(heads, RING, 1, nq, dtype=F32), vm(heads, 1, nq, dtype=F32),
        vm(heads, 1, nq, dtype=F32), vm(heads, RING, 1, nq, dtype=F32),
        vm(heads, RING, rows, HD), vm(heads, 3, rows, HD),
        vm(HD, nq, dtype=F32), vm(heads, RING, rows, HD), vm(heads, 3, rows, HD),
        vm(heads, CORES, RING, 2, rows, HD), vm(heads, RING, 2, rows, HD),
        vm(heads, 3, 2, rows, HD),
        vm(heads, RING, RING, CORES, wcols, HD), vm(heads, RING, RING, wcols, HD),
        vm(heads, 3, RING, wcols, HD), vm(heads, 3, wcols, HD), vm(heads, RING, wcols, HD),
        pltpu.SemaphoreType.DMA((nsem,)), pltpu.SemaphoreType.DMA((nsem,)),
    ]
    vmem = pl.BlockSpec(memory_space=pltpu.VMEM)

    def body(*refs):
        kernel((rows, heads, wcols, nsem), *refs)

    like = jax.ShapeDtypeStruct((rows, width), BF16)
    dq, dk, dv, gp = pl.pallas_call(
        body,
        out_shape=(like, like, like, jax.ShapeDtypeStruct((wcols, width), F32)),
        in_specs=[vmem] * 5,
        out_specs=(vmem,) * 4,
        scratch_shapes=scratch,
        compiler_params=pltpu.CompilerParams(
            collective_id=0, has_side_effects=True, vmem_limit_bytes=60 * 1024 * 1024),
        name="fused",
    )(queries, keys, values, grad_out, proj_weight.T)
    return dq, dk, dv, gp.T


def solution(mesh):
    spec = P("frame", "space")
    return jax.shard_map(
        local, mesh=mesh, in_specs=(spec,) * 4 + (P("space", "frame"),),
        out_specs=(spec,) * 3 + (P("space", "frame"),), check_vma=False)
```

```python
import functools
import math

import jax
import jax.numpy as jnp
from jax import lax
from jax.experimental import pallas as pl
from jax.experimental.pallas import tpu as pltpu
from jax.sharding import PartitionSpec as P

HD = 128
MESH = pl.DeviceIdType.MESH
F32 = jnp.float32
BF16 = jnp.bfloat16
RING = 4
CORES = 2
PAIR = 2


ORDER = (
    "Q01", "Q11", "W01", "W11", "K01", "Q21", "G1", "K11", "W21", "own", "K21", "K02", "Q02",
    "K12", "Q12", "W02", "K22", "W12", "K03", "K13", "K04", "Q22", "K23", "K14", "K24", "G2",
    "W22", "Q03", "T0", "L0", "Q13", "W03", "X01", "P0", "W13", "l01", "T1", "L1", "P1", "W23",
    "G3", "X02", "Q23", "T2", "L2", "l02", "P2", "X03", "N0", "l21", "X11", "l11", "X21", "O01",
    "X04", "G4", "A0", "D01", "gt", "O02", "X12", "l22", "N2", "l12", "O21", "N1", "O11", "X22",
    "D02", "X13", "O03", "J0", "Y01", "O22", "X14", "A1", "D11", "X23", "O12", "Y02", "X24", "A2",
    "D21", "D03", "R0", "u01", "O23", "J2", "Y21", "Y03", "D12", "O13", "J1", "Y22", "Y11", "Y04",
    "D22", "D13", "R1", "u11", "Y12", "Y23", "u02", "B0", "Y05", "D23", "Y13", "R2", "u21", "V01",
    "E01", "u12", "B1", "Y24", "Y06", "E11", "Y14", "E02", "V11", "V02", "u22", "B2", "E21",
    "Y25", "V03", "V21", "V12", "E12", "V22", "Y15", "V04", "V13", "E03", "E22", "V23", "Y26",
    "E13", "V14", "Y16", "V24", "E23",
)


def mm(a, b):
    return jnp.dot(a, b, preferred_element_type=F32)


def kernel(dims, q_ref, k_ref, v_ref, g_ref, w_ref, dq_ref, dk_ref, dv_ref, gp_ref, *scratch):
    rows, heads, wcols, nsem = dims
    (q4, kv8, g8, gt, wb, da, do4, qt, kt, vt, don, dsl, at, s_buf, p_buf, ot, l_in, u_out, l_out, u_in,
     ob, ol, dqt, dqb, dql, dkvb, dkvc, dkvl, gpb, gpc, gpx, gpz, gpr,
     send_sems, recv_sems) = scratch
    width = heads * HD
    nq = RING * rows
    kc = CORES * rows
    factor = 1.0 / math.sqrt(HD)
    c2 = factor * math.log2(math.e)

    f = lax.axis_index("frame")
    s = lax.axis_index("space")
    x, zh, core = f // 8, lax.rem(f // 2, 4), lax.rem(f, 2)
    zl, y = s // 4, lax.rem(s, 4)

    def around(i, k):
        return lax.rem(i + k, RING)

    def dev_f(xx, zz, cc):
        return {"frame": (xx * RING + zz) * CORES + cc}

    xs = [dev_f(around(x, k), zh, core) for k in range(4)]
    zs = [dev_f(x, around(zh, k), core) for k in range(4)]
    sib = dev_f(x, zh, 1 - core)
    ys = [{"space": zl * RING + around(y, k)} for k in range(4)]
    zsib = {"space": (1 - zl) * RING + y}

    partners = [zs[1], zs[3], xs[1], xs[3], ys[1], ys[3], sib, zsib]
    barrier = pltpu.get_barrier_semaphore()
    for other in partners:
        pl.semaphore_signal(barrier, inc=1, device_id=other, device_id_type=MESH)
    pl.semaphore_wait(barrier, len(partners))

    used = [0]
    pending = []

    def send(src, dst, device):
        n = used[0]
        used[0] += 1
        copy = pltpu.make_async_remote_copy(
            src_ref=src, dst_ref=dst, send_sem=send_sems.at[n], recv_sem=recv_sems.at[n],
            device_id=device, device_id_type=MESH)
        copy.start()
        pending.append(copy)
        return copy

    def gather(own, at, lo, hi, i, devs, forward=None):
        p, n, o = around(i, 1), around(i, 3), around(i, 2)
        first = [(send(src, dst, devs[1]), send(src, dst, devs[3])) for src, dst in own]
        fw = []
        if forward is not None:
            fw += [send(src, dst, forward) for src, dst in own]
        yield
        for c0, _ in first:
            c0.wait_recv()
        c2 = send(lo(n), lo(n), devs[1])
        if forward is not None:
            fw.append(send(at(n), at(n), forward))
        for _, c1 in first:
            c1.wait_recv()
        c3 = send(hi(p), hi(p), devs[3])
        if forward is not None:
            fw.append(send(at(p), at(p), forward))
        yield
        c2.wait_recv()
        c3.wait_recv()
        if forward is not None:
            fw.append(send(at(o), at(o), forward))
            yield
            for c in fw:
                c.wait_recv()

    def add_into(dst, landed):
        dst[...] = (dst[...].astype(F32) + landed[...].astype(F32)).astype(BF16)

    def scatter(blk, size, land, i, devs, out):
        h = size // 2
        p, n, o = around(i, 1), around(i, 3), around(i, 2)
        a0, b0 = land.at[0, 0:h], land.at[0, h:size]
        from_n, from_p = land.at[1], land.at[2]
        c0 = send(blk(o, 0, h), a0, devs[1])
        c1 = send(blk(o, h, size), b0, devs[3])
        c2 = send(blk(p, h, size), land.at[1, h:size], devs[1])
        c3 = send(blk(n, 0, h), land.at[2, 0:h], devs[3])
        yield
        c0.wait_recv()
        add_into(blk(p, 0, h), a0)
        c4 = send(blk(p, 0, h), land.at[1, 0:h], devs[1])
        c1.wait_recv()
        add_into(blk(n, h, size), b0)
        c5 = send(blk(n, h, size), land.at[2, h:size], devs[3])
        yield
        for c in (c2, c3, c4, c5):
            c.wait_recv()
        out(blk(i, 0, size)[...].astype(F32) + from_n[...].astype(F32) + from_p[...].astype(F32))

    def spread(src, land):
        copies = [send(src, land.at[zh], zs[k]) for k in (1, 3, 2)]
        yield
        for c in copies:
            c.wait_recv()

    def pump(*flows):
        for flow in flows:
            next(flow, None)

    def cols(h):
        return slice(h * HD, (h + 1) * HD)

    half = rows // 2
    hw = wcols // 2
    H = range(heads)

    def q_flow(h):
        own = [(q_ref.at[:, cols(h)], q4.at[h, zh])]
        return gather(own, lambda j: q4.at[h, j], lambda j: q4.at[h, j, 0:half],
                      lambda j: q4.at[h, j, half:rows], zh, zs)

    def kv_flow(h):
        own = [(k_ref.at[:, cols(h)], kv8.at[h, x, core, 0]),
               (v_ref.at[:, cols(h)], kv8.at[h, x, core, 1])]
        return gather(own, lambda j: kv8.at[h, j, core], lambda j: kv8.at[h, j, core, 0],
                      lambda j: kv8.at[h, j, core, 1], x, xs, sib)

    def wz_flow(h):
        own = [(w_ref.at[:, cols(h)], wb.at[h, x, zh, core])]
        return gather(own, lambda j: wb.at[h, x, j, core], lambda j: wb.at[h, x, j, core, 0:hw],
                      lambda j: wb.at[h, x, j, core, hw:wcols], zh, zs)

    def wx_flow(h):
        own = [(wb.at[h, x, :, core], wb.at[h, x, :, core])]
        return gather(own, lambda j: wb.at[h, j, :, core], lambda j: wb.at[h, j, 0:2, core],
                      lambda j: wb.at[h, j, 2:4, core], x, xs, sib)

    def g_flow():
        c = send(g_ref, g8.at[zl, y], zsib)
        yield
        c.wait_recv()
        own = [(g8.at[:, y], g8.at[:, y])]
        yield from gather(own, lambda j: g8.at[:, j], lambda j: g8.at[0, j],
                          lambda j: g8.at[1, j], y, ys)

    def do_flow(h):
        own = [(da.at[h], do4.at[h, zh])]
        return gather(own, lambda j: do4.at[h, j], lambda j: do4.at[h, j, 0:half],
                      lambda j: do4.at[h, j, half:rows], zh, zs)

    def turn(h):
        qt[h] = q4[h].reshape(nq, HD).T
        for j in range(RING):
            kt[h, j] = kv8[h, j, :, 0].reshape(kc, HD).T
            vt[h, j] = kv8[h, j, :, 1].reshape(kc, HD).T

    tops = {}

    def logits_pass(h):
        def body(j, m8):
            sc = mm(kv8[h, j, :, 0].reshape(kc, HD), qt[h])
            s_buf[j] = sc
            return jnp.maximum(m8, jnp.max(sc.reshape(kc // 8, 8, nq), axis=0))
        m8 = lax.fori_loop(0, RING, body, jnp.full((8, nq), -jnp.inf, F32))
        tops[h] = jnp.max(m8, axis=0, keepdims=True)

    def probs_pass(h):
        m = tops[h]
        ot[h] = jnp.zeros((HD, nq), F32)

        def body(j, l8):
            pr = jnp.exp2((s_buf[j] - m) * c2)
            low = pr.astype(BF16)
            p_buf[h, j] = low
            ot[h] += mm(vt[h, j], low)
            return l8 + jnp.sum(pr.reshape(kc // 8, 8, nq), axis=0)
        l8 = lax.fori_loop(0, RING, body, jnp.zeros((8, nq), F32))
        l_out[h] = m * c2 + jnp.log2(jnp.sum(l8, axis=0, keepdims=True))

    scales = {}

    def normalise(h):
        l_in[h, zh] = l_out[h]
        ls = [l_in[h, j] for j in range(RING)]
        top = jnp.maximum(jnp.maximum(ls[0], ls[1]), jnp.maximum(ls[2], ls[3]))
        total = sum(jnp.exp2(v - top) for v in ls)
        scales[h] = jnp.exp2(tops[h] * c2 - (top + jnp.log2(total)))
        ob[h] = (ot[h] * scales[h]).T.astype(BF16).reshape(RING, rows, HD)

    def o_flow(h):
        def keep(value):
            at[h] = value.astype(BF16)
        return scatter(lambda j, lo, hi: ob.at[h, j, lo:hi], rows, ol.at[h], zh, zs, keep)

    def grad_attn(h):
        acc = jnp.zeros((rows, HD), F32)
        for t in range(PAIR * RING):
            block = wb[h, t // 2, 2 * (t % 2):2 * (t % 2) + 2].reshape(width, HD)
            acc = acc + mm(g8[t // RING, t % RING], block)
        low = acc.astype(BF16)
        da[h] = low
        do4[h, zh] = low

    def row_terms(h):
        scaled = do4[h].reshape(nq, HD).astype(F32).T * scales[h]
        u_out[h] = jnp.sum(scaled * ot[h], axis=0, keepdims=True)
        dsl[h] = scaled.astype(BF16)
        don[h] = scaled.T.astype(BF16)

    def backward(h):
        u_in[h, zh] = u_out[h]
        dl = (u_in[h, 0] + u_in[h, 1] + u_in[h, 2] + u_in[h, 3]) * scales[h]
        dqt[...] = jnp.zeros_like(dqt)

        def body(j, unused):
            dp = mm(kv8[h, j, :, 1].reshape(kc, HD), dsl[h])
            pr = p_buf[h, j]
            dlog = (pr.astype(F32) * (dp - dl)).astype(BF16)
            dkvb[h, :, j, 1] = mm(pr, don[h]).astype(BF16).reshape(CORES, rows, HD)
            dkvb[h, :, j, 0] = (factor * mm(dlog, q4[h].reshape(nq, HD))).astype(
                BF16).reshape(CORES, rows, HD)
            dqt[...] += mm(kt[h, j], dlog)
            return unused
        lax.fori_loop(0, RING, body, 0)
        dqb[h] = (factor * dqt[...]).T.astype(BF16).reshape(RING, rows, HD)

    def proj(h):
        for t in range(PAIR * RING):
            part = mm(gt[t], at[h])
            gpb[h, t // 2, 2 * (t % 2):2 * (t % 2) + 2] = part.astype(BF16).reshape(
                2, CORES, wcols, HD)

    def dkv_flow(h):
        c = send(dkvb.at[h, 1 - core], dkvc.at[h], sib)
        yield
        c.wait_recv()
        add_into(dkvb.at[h, core], dkvc.at[h])

        def write(value):
            dk_ref[:, cols(h)] = value[0].astype(BF16)
            dv_ref[:, cols(h)] = value[1].astype(BF16)
        yield from scatter(lambda j, lo, hi: dkvb.at[h, core, j, lo:hi], 2, dkvl.at[h], x, xs,
                           write)

    def dq_flow(h):
        def write(value):
            dq_ref[:, cols(h)] = value.astype(BF16)
        return scatter(lambda j, lo, hi: dqb.at[h, j, lo:hi], rows, dql.at[h], zh, zs, write)

    def gp_flow(h):
        c = send(gpb.at[h, :, :, 1 - core], gpc.at[h], sib)
        yield
        c.wait_recv()
        for j in range(RING):
            add_into(gpb.at[h, j, :, core], gpc.at[h, j])

        def keep(value):
            gpr[h] = value.astype(BF16)
        yield from scatter(lambda j, lo, hi: gpb.at[h, j, lo:hi, core], RING, gpx.at[h], x, xs,
                           keep)

        def final(value):
            gp_ref[:, cols(h)] = value
        yield from scatter(lambda j, lo, hi: gpr.at[h, j, lo:hi], wcols, gpz.at[h], zh, zs, final)

    QZ, KV, WZ = [q_flow(h) for h in H], [kv_flow(h) for h in H], [wz_flow(h) for h in H]
    WX, DZ, OZ = [wx_flow(h) for h in H], [do_flow(h) for h in H], [o_flow(h) for h in H]
    LX = [spread(l_out.at[h], l_in.at[h]) for h in H]
    UX = [spread(u_out.at[h], u_in.at[h]) for h in H]
    DK, DQ, GP = [dkv_flow(h) for h in H], [dq_flow(h) for h in H], [gp_flow(h) for h in H]
    G = g_flow()
    def own_blocks():
        g8[zl, y] = g_ref[...]
        for h in H:
            q4[h, zh] = q_ref[:, cols(h)]
            kv8[h, x, core, 0] = k_ref[:, cols(h)]
            kv8[h, x, core, 1] = v_ref[:, cols(h)]
            wb[h, x, zh, core] = w_ref[:, cols(h)]

    def turn_g():
        for t in range(PAIR * RING):
            gt[t] = g8[t // RING, t % RING].T

    steps = {"own": own_blocks, "gt": turn_g}
    flows = {"G": g_flow()}
    for h in H:
        for name, make in (("Q", q_flow), ("K", kv_flow), ("W", wz_flow), ("X", wx_flow),
                           ("D", do_flow), ("O", o_flow), ("V", dkv_flow), ("E", dq_flow),
                           ("Y", gp_flow)):
            flows[name + str(h)] = make(h)
        flows["l" + str(h)] = spread(l_out.at[h], l_in.at[h])
        flows["u" + str(h)] = spread(u_out.at[h], u_in.at[h])
        for name, call in (("T", turn), ("L", logits_pass), ("P", probs_pass), ("N", normalise),
                           ("A", grad_attn), ("R", row_terms), ("B", backward), ("J", proj)):
            steps[name + str(h)] = functools.partial(call, h)
    for name in ORDER:
        if name in steps:
            steps[name]()
        else:
            next(flows[name[:-1]], None)
    for flow in flows.values():
        assert next(flow, flow) is flow
    for c in pending:
        c.wait_send()
    assert used[0] <= nsem, used[0]


def keep(*refs):
    for src, dst in zip(refs[:4], refs[4:]):
        dst[...] = src[...]


def local(queries, keys, values, grad_out, proj_weight):
    rows, width = queries.shape
    heads = width // HD
    wcols = proj_weight.shape[1]
    nq, kc = RING * rows, CORES * rows
    nsem = 240

    def vm(*shape, dtype=BF16):
        return pltpu.VMEM(shape, dtype)

    scratch = [
        vm(heads, RING, rows, HD), vm(heads, RING, CORES, 2, rows, HD),
        vm(PAIR, RING, rows, width), vm(PAIR * RING, width, rows),
        vm(heads, RING, RING, CORES, wcols, HD),
        vm(heads, rows, HD), vm(heads, RING, rows, HD),
        vm(heads, HD, nq), vm(heads, RING, HD, kc), vm(heads, RING, HD, kc),
        vm(heads, nq, HD), vm(heads, HD, nq), vm(heads, rows, HD),
        vm(RING, kc, nq, dtype=F32), vm(heads, RING, kc, nq), vm(heads, HD, nq, dtype=F32),
        vm(heads, RING, 1, nq, dtype=F32), vm(heads, 1, nq, dtype=F32),
        vm(heads, 1, nq, dtype=F32), vm(heads, RING, 1, nq, dtype=F32),
        vm(heads, RING, rows, HD), vm(heads, 3, rows, HD),
        vm(HD, nq, dtype=F32), vm(heads, RING, rows, HD), vm(heads, 3, rows, HD),
        vm(heads, CORES, RING, 2, rows, HD), vm(heads, RING, 2, rows, HD),
        vm(heads, 3, 2, rows, HD),
        vm(heads, RING, RING, CORES, wcols, HD), vm(heads, RING, RING, wcols, HD),
        vm(heads, 3, RING, wcols, HD), vm(heads, 3, wcols, HD), vm(heads, RING, wcols, HD),
        pltpu.SemaphoreType.DMA((nsem,)), pltpu.SemaphoreType.DMA((nsem,)),
    ]
    vmem = pl.BlockSpec(memory_space=pltpu.VMEM)

    def body(*refs):
        kernel((rows, heads, wcols, nsem), *refs)

    like = jax.ShapeDtypeStruct((rows, width), BF16)
    dq, dk, dv, gp = pl.pallas_call(
        body,
        out_shape=(like, like, like, jax.ShapeDtypeStruct((wcols, width), F32)),
        in_specs=[vmem] * 5,
        out_specs=(vmem,) * 4,
        scratch_shapes=scratch,
        compiler_params=pltpu.CompilerParams(
            collective_id=0, has_side_effects=True, vmem_limit_bytes=60 * 1024 * 1024),
        name="fused",
    )(queries, keys, values, grad_out, proj_weight.T)
    dq, dk, dv, gp = pl.pallas_call(
        keep,
        out_shape=(like, like, like, jax.ShapeDtypeStruct((wcols, width), F32)),
        in_specs=[vmem] * 4,
        out_specs=(vmem,) * 4,
        name="keep",
    )(dq, dk, dv, gp)
    return dq, dk, dv, gp.T


def solution(mesh):
    spec = P("frame", "space")
    return jax.shard_map(
        local, mesh=mesh, in_specs=(spec,) * 4 + (P("space", "frame"),),
        out_specs=(spec,) * 3 + (P("space", "frame"),), check_vma=False)
```

```python
import functools
import math

import jax
import jax.numpy as jnp
from jax import lax
from jax.experimental import pallas as pl
from jax.experimental.pallas import tpu as pltpu
from jax.sharding import PartitionSpec as P

HD = 128
MESH = pl.DeviceIdType.MESH
F32 = jnp.float32
BF16 = jnp.bfloat16
RING = 4
CORES = 2
PAIR = 2


ORDER = (
    "W01", "K11", "K01", "W11", "G1", "W02", "Q01", "K12", "K02", "W12", "G2", "W21", "K21",
    "Q11", "W03", "X01", "Q02", "W13", "K13", "Q21", "X11", "K03", "W22", "X02", "Q12", "K22",
    "K04", "G3", "K14", "Q03", "T0", "L0", "P0", "l01", "W23", "X21", "Q22", "X03", "N0", "O01",
    "K23", "Q13", "X12", "T1", "L1", "G4", "X04", "A0", "D01", "P1", "Q23", "l11", "X22", "l02",
    "M0", "O02", "N1", "K24", "X13", "O11", "T2", "L2", "gt", "D02", "X14", "A1", "X23", "D11",
    "P2", "O03", "J0", "l12", "l21", "N2", "M1", "Y01", "X24", "O12", "A2", "D21", "D03", "R0",
    "u01", "D12", "Y02", "O21", "O13", "J1", "Y11", "l22", "D22", "M2", "Y03", "D13", "R1", "u11",
    "Y12", "u02", "O22", "B0", "V01", "D23", "R2", "u21", "Y04", "E01", "Y13", "O23", "J2", "Y21",
    "u12", "B1", "V11", "Y22", "V02", "Y14", "u22", "E11", "B2", "Y23", "V21", "E02", "V12",
    "E21", "Y15", "V22", "Y24", "Y05", "V03", "E22", "E12", "V13", "V23", "Y25", "E23", "V14",
    "V24", "Y16", "Y06", "E03", "E13", "V04", "Y26",
)


def mm(a, b):
    return jnp.dot(a, b, preferred_element_type=F32)


def kernel(dims, q_ref, k_ref, v_ref, g_ref, w_ref, dq_ref, dk_ref, dv_ref, gp_ref, *scratch):
    rows, heads, wcols, nsem = dims
    (q4, kv8, g8, gt, wb, da, do4, qt, kt, vt, don, dsl, at, wc, s_buf, p_buf, ot, l_in, u_out, l_out, u_in,
     ob, ol, dqt, dqb, dql, dkvb, dkvc, dkvl, gpb, gpc, gpx, gpz, gpr,
     send_sems, recv_sems) = scratch
    width = heads * HD
    nq = RING * rows
    kc = CORES * rows
    factor = 1.0 / math.sqrt(HD)
    c2 = factor * math.log2(math.e)

    f = lax.axis_index("frame")
    s = lax.axis_index("space")
    x, zh, core = f // 8, lax.rem(f // 2, 4), lax.rem(f, 2)
    zl, y = s // 4, lax.rem(s, 4)

    def around(i, k):
        return lax.rem(i + k, RING)

    def dev_f(xx, zz, cc):
        return {"frame": (xx * RING + zz) * CORES + cc}

    xs = [dev_f(around(x, k), zh, core) for k in range(4)]
    zs = [dev_f(x, around(zh, k), core) for k in range(4)]
    sib = dev_f(x, zh, 1 - core)
    ys = [{"space": zl * RING + around(y, k)} for k in range(4)]
    zsib = {"space": (1 - zl) * RING + y}

    partners = [zs[1], zs[3], xs[1], xs[3], ys[1], ys[3], sib, zsib]
    barrier = pltpu.get_barrier_semaphore()
    for other in partners:
        pl.semaphore_signal(barrier, inc=1, device_id=other, device_id_type=MESH)
    g8[zl, y] = g_ref[...]
    for h in range(heads):
        part = slice(h * HD, (h + 1) * HD)
        q4[h, zh] = q_ref[:, part]
        kv8[h, x, core, 0] = k_ref[:, part]
        kv8[h, x, core, 1] = v_ref[:, part]
        wb[h, x, zh, core] = w_ref[:, part]
    pl.semaphore_wait(barrier, len(partners))

    used = [0]
    pending = []

    def send(src, dst, device):
        n = used[0]
        used[0] += 1
        copy = pltpu.make_async_remote_copy(
            src_ref=src, dst_ref=dst, send_sem=send_sems.at[n], recv_sem=recv_sems.at[n],
            device_id=device, device_id_type=MESH)
        copy.start()
        pending.append(copy)
        return copy

    def gather(own, at, lo, hi, i, devs, forward=None):
        p, n, o = around(i, 1), around(i, 3), around(i, 2)
        first = [(send(src, dst, devs[1]), send(src, dst, devs[3])) for src, dst in own]
        fw = []
        if forward is not None:
            fw += [send(src, dst, forward) for src, dst in own]
        yield
        for c0, _ in first:
            c0.wait_recv()
        c2 = send(lo(n), lo(n), devs[1])
        if forward is not None:
            fw.append(send(at(n), at(n), forward))
        for _, c1 in first:
            c1.wait_recv()
        c3 = send(hi(p), hi(p), devs[3])
        if forward is not None:
            fw.append(send(at(p), at(p), forward))
        yield
        c2.wait_recv()
        c3.wait_recv()
        if forward is not None:
            fw.append(send(at(o), at(o), forward))
            yield
            for c in fw:
                c.wait_recv()

    def add_into(dst, landed):
        dst[...] = (dst[...].astype(F32) + landed[...].astype(F32)).astype(BF16)

    def scatter(blk, size, land, i, devs, out):
        h = size // 2
        p, n, o = around(i, 1), around(i, 3), around(i, 2)
        a0, b0 = land.at[0, 0:h], land.at[0, h:size]
        from_n, from_p = land.at[1], land.at[2]
        c0 = send(blk(o, 0, h), a0, devs[1])
        c1 = send(blk(o, h, size), b0, devs[3])
        c2 = send(blk(p, h, size), land.at[1, h:size], devs[1])
        c3 = send(blk(n, 0, h), land.at[2, 0:h], devs[3])
        yield
        c0.wait_recv()
        add_into(blk(p, 0, h), a0)
        c4 = send(blk(p, 0, h), land.at[1, 0:h], devs[1])
        c1.wait_recv()
        add_into(blk(n, h, size), b0)
        c5 = send(blk(n, h, size), land.at[2, h:size], devs[3])
        yield
        for c in (c2, c3, c4, c5):
            c.wait_recv()
        out(blk(i, 0, size)[...].astype(F32) + from_n[...].astype(F32) + from_p[...].astype(F32))

    def spread(src, land):
        copies = [send(src, land.at[zh], zs[k]) for k in (1, 3, 2)]
        yield
        for c in copies:
            c.wait_recv()

    def pump(*flows):
        for flow in flows:
            next(flow, None)

    def cols(h):
        return slice(h * HD, (h + 1) * HD)

    half = rows // 2
    hw = wcols // 2
    H = range(heads)

    def q_flow(h):
        own = [(q_ref.at[:, cols(h)], q4.at[h, zh])]
        return gather(own, lambda j: q4.at[h, j], lambda j: q4.at[h, j, 0:half],
                      lambda j: q4.at[h, j, half:rows], zh, zs)

    def kv_flow(h):
        own = [(k_ref.at[:, cols(h)], kv8.at[h, x, core, 0]),
               (v_ref.at[:, cols(h)], kv8.at[h, x, core, 1])]
        return gather(own, lambda j: kv8.at[h, j, core], lambda j: kv8.at[h, j, core, 0],
                      lambda j: kv8.at[h, j, core, 1], x, xs, sib)

    def wz_flow(h):
        own = [(w_ref.at[:, cols(h)], wb.at[h, x, zh, core])]
        return gather(own, lambda j: wb.at[h, x, j, core], lambda j: wb.at[h, x, j, core, 0:hw],
                      lambda j: wb.at[h, x, j, core, hw:wcols], zh, zs)

    def wx_flow(h):
        own = [(wb.at[h, x, :, core], wb.at[h, x, :, core])]
        return gather(own, lambda j: wb.at[h, j, :, core], lambda j: wb.at[h, j, 0:2, core],
                      lambda j: wb.at[h, j, 2:4, core], x, xs, sib)

    def g_flow():
        c = send(g_ref, g8.at[zl, y], zsib)
        yield
        c.wait_recv()
        own = [(g8.at[:, y], g8.at[:, y])]
        yield from gather(own, lambda j: g8.at[:, j], lambda j: g8.at[0, j],
                          lambda j: g8.at[1, j], y, ys)

    def do_flow(h):
        own = [(da.at[h], do4.at[h, zh])]
        return gather(own, lambda j: do4.at[h, j], lambda j: do4.at[h, j, 0:half],
                      lambda j: do4.at[h, j, half:rows], zh, zs)

    def turn(h):
        qt[h] = q4[h].reshape(nq, HD).T
        for j in range(RING):
            kt[h, j] = kv8[h, j, :, 0].reshape(kc, HD).T
            vt[h, j] = kv8[h, j, :, 1].reshape(kc, HD).T

    tops, sums = {}, {}

    def logits_pass(h):
        def body(j, m8):
            sc = mm(kv8[h, j, :, 0].reshape(kc, HD), qt[h])
            s_buf[j] = sc
            return jnp.maximum(m8, jnp.max(sc.reshape(kc // 8, 8, nq), axis=0))
        m8 = lax.fori_loop(0, RING, body, jnp.full((8, nq), -jnp.inf, F32))
        tops[h] = jnp.max(m8, axis=0, keepdims=True)

    def probs_pass(h):
        m = tops[h]
        ot[h] = jnp.zeros((HD, nq), F32)

        def body(j, l8):
            pr = jnp.exp2((s_buf[j] - m) * c2)
            low = pr.astype(BF16)
            p_buf[h, j] = low
            ot[h] += mm(vt[h, j], low)
            return l8 + jnp.sum(pr.reshape(kc // 8, 8, nq), axis=0)
        l8 = lax.fori_loop(0, RING, body, jnp.zeros((8, nq), F32))
        sums[h] = jnp.sum(l8, axis=0, keepdims=True)
        l_out[h] = m * c2 + jnp.log2(sums[h])

    scales = {}

    def partial_out(h):
        ob[h] = (ot[h] / sums[h]).T.astype(BF16).reshape(RING, rows, HD)

    def weigh(h):
        l_in[h, zh] = l_out[h]
        ls = [l_in[h, around(zh, k)] for k in range(RING)]
        top = jnp.maximum(jnp.maximum(ls[0], ls[1]), jnp.maximum(ls[2], ls[3]))
        full = top + jnp.log2(sum(jnp.exp2(v - top) for v in ls))
        scales[h] = jnp.exp2(tops[h] * c2 - full)
        table = jnp.concatenate(
            [jnp.exp2(ls[k] - full) for k in (0, 3, 1)] + [jnp.zeros((5, nq), F32)], axis=0)
        wc[h] = table.T.reshape(RING, rows, 8)

    def o_flow(h):
        p, n, o = around(zh, 1), around(zh, 3), around(zh, 2)
        blk = ob.at[h]
        land = ol.at[h]
        lo, hi = slice(0, half), slice(half, rows)

        def w(j, part, k):
            return wc[h, j, part, k:k + 1]

        def wide(ref):
            return ref[...].astype(F32)
        c0 = send(blk.at[o, lo], land.at[0, lo], zs[1])
        c1 = send(blk.at[o, hi], land.at[0, hi], zs[3])
        c2_ = send(blk.at[p, hi], land.at[1, hi], zs[1])
        c3 = send(blk.at[n, lo], land.at[2, lo], zs[3])
        yield
        c0.wait_recv()
        mine = blk.at[p, lo]
        mine[...] = (wide(mine) * w(p, lo, 0) + wide(land.at[0, lo]) * w(p, lo, 1)).astype(BF16)
        c4 = send(mine, land.at[1, lo], zs[1])
        c1.wait_recv()
        mine = blk.at[n, hi]
        mine[...] = (wide(mine) * w(n, hi, 0) + wide(land.at[0, hi]) * w(n, hi, 2)).astype(BF16)
        c5 = send(mine, land.at[2, hi], zs[3])
        yield
        for c in (c2_, c3, c4, c5):
            c.wait_recv()
        at[h, lo] = (wide(blk.at[zh, lo]) * w(zh, lo, 0) + wide(land.at[1, lo])
                     + wide(land.at[2, lo]) * w(zh, lo, 2)).astype(BF16)
        at[h, hi] = (wide(blk.at[zh, hi]) * w(zh, hi, 0) + wide(land.at[1, hi]) * w(zh, hi, 1)
                     + wide(land.at[2, hi])).astype(BF16)

    def grad_attn(h):
        acc = jnp.zeros((rows, HD), F32)
        for t in range(PAIR * RING):
            block = wb[h, t // 2, 2 * (t % 2):2 * (t % 2) + 2].reshape(width, HD)
            acc = acc + mm(g8[t // RING, t % RING], block)
        low = acc.astype(BF16)
        da[h] = low
        do4[h, zh] = low

    def row_terms(h):
        scaled = do4[h].reshape(nq, HD).astype(F32).T * scales[h]
        u_out[h] = jnp.sum(scaled * ot[h], axis=0, keepdims=True)
        dsl[h] = scaled.astype(BF16)
        don[h] = scaled.T.astype(BF16)

    def backward(h):
        u_in[h, zh] = u_out[h]
        dl = (u_in[h, 0] + u_in[h, 1] + u_in[h, 2] + u_in[h, 3]) * scales[h]
        dqt[...] = jnp.zeros_like(dqt)

        def body(j, unused):
            dp = mm(kv8[h, j, :, 1].reshape(kc, HD), dsl[h])
            pr = p_buf[h, j]
            dlog = (pr.astype(F32) * (dp - dl)).astype(BF16)
            dkvb[h, :, j, 1] = mm(pr, don[h]).astype(BF16).reshape(CORES, rows, HD)
            dkvb[h, :, j, 0] = (factor * mm(dlog, q4[h].reshape(nq, HD))).astype(
                BF16).reshape(CORES, rows, HD)
            dqt[...] += mm(kt[h, j], dlog)
            return unused
        lax.fori_loop(0, RING, body, 0)
        dqb[h] = (factor * dqt[...]).T.astype(BF16).reshape(RING, rows, HD)

    def proj(h):
        for t in range(PAIR * RING):
            part = mm(gt[t], at[h])
            gpb[h, t // 2, 2 * (t % 2):2 * (t % 2) + 2] = part.astype(BF16).reshape(
                2, CORES, wcols, HD)

    def dkv_flow(h):
        c = send(dkvb.at[h, 1 - core], dkvc.at[h], sib)
        yield
        c.wait_recv()
        add_into(dkvb.at[h, core], dkvc.at[h])

        def write(value):
            dk_ref[:, cols(h)] = value[0].astype(BF16)
            dv_ref[:, cols(h)] = value[1].astype(BF16)
        yield from scatter(lambda j, lo, hi: dkvb.at[h, core, j, lo:hi], 2, dkvl.at[h], x, xs,
                           write)

    def dq_flow(h):
        def write(value):
            dq_ref[:, cols(h)] = value.astype(BF16)
        return scatter(lambda j, lo, hi: dqb.at[h, j, lo:hi], rows, dql.at[h], zh, zs, write)

    def gp_flow(h):
        c = send(gpb.at[h, :, :, 1 - core], gpc.at[h], sib)
        yield
        c.wait_recv()
        for j in range(RING):
            add_into(gpb.at[h, j, :, core], gpc.at[h, j])

        def keep(value):
            gpr[h] = value.astype(BF16)
        yield from scatter(lambda j, lo, hi: gpb.at[h, j, lo:hi, core], RING, gpx.at[h], x, xs,
                           keep)

        def final(value):
            gp_ref[:, cols(h)] = value
        yield from scatter(lambda j, lo, hi: gpr.at[h, j, lo:hi], wcols, gpz.at[h], zh, zs, final)

    QZ, KV, WZ = [q_flow(h) for h in H], [kv_flow(h) for h in H], [wz_flow(h) for h in H]
    WX, DZ, OZ = [wx_flow(h) for h in H], [do_flow(h) for h in H], [o_flow(h) for h in H]
    LX = [spread(l_out.at[h], l_in.at[h]) for h in H]
    UX = [spread(u_out.at[h], u_in.at[h]) for h in H]
    DK, DQ, GP = [dkv_flow(h) for h in H], [dq_flow(h) for h in H], [gp_flow(h) for h in H]
    G = g_flow()
    def turn_g():
        for t in range(PAIR * RING):
            gt[t] = g8[t // RING, t % RING].T

    steps = {"gt": turn_g}
    flows = {"G": g_flow()}
    for h in H:
        for name, make in (("Q", q_flow), ("K", kv_flow), ("W", wz_flow), ("X", wx_flow),
                           ("D", do_flow), ("O", o_flow), ("V", dkv_flow), ("E", dq_flow),
                           ("Y", gp_flow)):
            flows[name + str(h)] = make(h)
        flows["l" + str(h)] = spread(l_out.at[h], l_in.at[h])
        flows["u" + str(h)] = spread(u_out.at[h], u_in.at[h])
        for name, call in (("T", turn), ("L", logits_pass), ("P", probs_pass), ("N", partial_out), ("M", weigh),
                           ("A", grad_attn), ("R", row_terms), ("B", backward), ("J", proj)):
            steps[name + str(h)] = functools.partial(call, h)
    for name in ORDER:
        if name in steps:
            steps[name]()
        else:
            next(flows[name[:-1]], None)
    for flow in flows.values():
        assert next(flow, flow) is flow
    for c in pending:
        c.wait_send()
    assert used[0] <= nsem, used[0]


def keep(*refs):
    for src, dst in zip(refs[:4], refs[4:]):
        dst[...] = src[...]


def local(queries, keys, values, grad_out, proj_weight):
    rows, width = queries.shape
    heads = width // HD
    wcols = proj_weight.shape[1]
    nq, kc = RING * rows, CORES * rows
    nsem = 240

    def vm(*shape, dtype=BF16):
        return pltpu.VMEM(shape, dtype)

    scratch = [
        vm(heads, RING, rows, HD), vm(heads, RING, CORES, 2, rows, HD),
        vm(PAIR, RING, rows, width), vm(PAIR * RING, width, rows),
        vm(heads, RING, RING, CORES, wcols, HD),
        vm(heads, rows, HD), vm(heads, RING, rows, HD),
        vm(heads, HD, nq), vm(heads, RING, HD, kc), vm(heads, RING, HD, kc),
        vm(heads, nq, HD), vm(heads, HD, nq), vm(heads, rows, HD),
        vm(heads, RING, rows, 8, dtype=F32),
        vm(RING, kc, nq, dtype=F32), vm(heads, RING, kc, nq), vm(heads, HD, nq, dtype=F32),
        vm(heads, RING, 1, nq, dtype=F32), vm(heads, 1, nq, dtype=F32),
        vm(heads, 1, nq, dtype=F32), vm(heads, RING, 1, nq, dtype=F32),
        vm(heads, RING, rows, HD), vm(heads, 3, rows, HD),
        vm(HD, nq, dtype=F32), vm(heads, RING, rows, HD), vm(heads, 3, rows, HD),
        vm(heads, CORES, RING, 2, rows, HD), vm(heads, RING, 2, rows, HD),
        vm(heads, 3, 2, rows, HD),
        vm(heads, RING, RING, CORES, wcols, HD), vm(heads, RING, RING, wcols, HD),
        vm(heads, 3, RING, wcols, HD), vm(heads, 3, wcols, HD), vm(heads, RING, wcols, HD),
        pltpu.SemaphoreType.DMA((nsem,)), pltpu.SemaphoreType.DMA((nsem,)),
    ]
    vmem = pl.BlockSpec(memory_space=pltpu.VMEM)

    def body(*refs):
        kernel((rows, heads, wcols, nsem), *refs)

    like = jax.ShapeDtypeStruct((rows, width), BF16)
    dq, dk, dv, gp = pl.pallas_call(
        body,
        out_shape=(like, like, like, jax.ShapeDtypeStruct((wcols, width), F32)),
        in_specs=[vmem] * 5,
        out_specs=(vmem,) * 4,
        scratch_shapes=scratch,
        compiler_params=pltpu.CompilerParams(
            collective_id=0, has_side_effects=True, vmem_limit_bytes=60 * 1024 * 1024),
        name="fused",
    )(queries, keys, values, grad_out, proj_weight.T)
    dq, dk, dv, gp = pl.pallas_call(
        keep,
        out_shape=(like, like, like, jax.ShapeDtypeStruct((wcols, width), F32)),
        in_specs=[vmem] * 4,
        out_specs=(vmem,) * 4,
        name="keep",
    )(dq, dk, dv, gp)
    return dq, dk, dv, gp.T


def solution(mesh):
    spec = P("frame", "space")
    return jax.shard_map(
        local, mesh=mesh, in_specs=(spec,) * 4 + (P("space", "frame"),),
        out_specs=(spec,) * 3 + (P("space", "frame"),), check_vma=False)
```

```python
import functools
import math

import jax
import jax.numpy as jnp
from jax import lax
from jax.experimental import pallas as pl
from jax.experimental.pallas import tpu as pltpu
from jax.sharding import PartitionSpec as P

HD = 128
MESH = pl.DeviceIdType.MESH
F32 = jnp.float32
BF16 = jnp.bfloat16
RING = 4
CORES = 2
PAIR = 2


ORDER = (
    "W01", "K11", "W11", "G1", "K01", "K21", "W02", "Q01", "K12", "W12", "W21", "Q11",
    "G2", "K02", "W03", "X01", "Q02", "K22", "Q21", "W13", "X11", "K13", "W22", "K03", "X02",
    "Q12", "K14", "K04", "G3", "Q03", "T0", "L0", "P0", "X12", "Q22", "N0", "X03", "l01", "W23",
    "O01", "X21", "Q13", "T1", "L1", "G4", "X04", "A0", "D01", "K23", "P1", "X13", "N1", "l11",
    "O11", "Q23", "K24", "l02", "M0", "O02", "X14", "X22", "T2", "A1", "D11", "L2", "D02", "P2",
    "l12", "M1", "O12", "l21", "N2", "O21", "O03", "X23", "gt", "J0", "Y01", "D12", "X24", "D03",
    "R0", "A2", "u01", "D21", "O13", "J1", "Y11", "Y02", "l22", "M2", "D13", "R1", "O22", "u11",
    "Y12", "u02", "D22", "B0", "E01", "Y13", "Y03", "O23", "J2", "Y21", "D23", "R2", "u21", "V01",
    "u12", "B1", "V11", "E02", "Y22", "Y04", "E11", "u22", "B2", "Y23", "V21", "E21", "V02",
    "Y05", "Y14", "V12", "Y24", "V22", "E22", "E12", "Y06", "V13", "Y15", "V03", "Y25", "V23",
    "E03", "E23", "V14", "V04", "Y16", "E13", "Y26", "V24",
)


def mm(a, b):
    return jnp.dot(a, b, preferred_element_type=F32)


def kernel(dims, q_ref, k_ref, v_ref, g_ref, w_ref, dq_ref, dk_ref, dv_ref, gp_ref, *scratch):
    rows, heads, wcols, nsem = dims
    (q4, kv8, g8, gt, wb, da, do4, qt, kt, vt, don, dsl, at, wc, s_buf, p_buf, ot, l_in, u_out, l_out, u_in,
     ob, ol, dqt, dqb, dql, dkvb, dkvc, dkvl, gpb, gpc, gpx, gpz, gpr,
     load_sems, send_sems, recv_sems) = scratch
    width = heads * HD
    nq = RING * rows
    kc = CORES * rows
    factor = 1.0 / math.sqrt(HD)
    c2 = factor * math.log2(math.e)

    f = lax.axis_index("frame")
    s = lax.axis_index("space")
    x, zh, core = f // 8, lax.rem(f // 2, 4), lax.rem(f, 2)
    zl, y = s // 4, lax.rem(s, 4)

    def around(i, k):
        return lax.rem(i + k, RING)

    def dev_f(xx, zz, cc):
        return {"frame": (xx * RING + zz) * CORES + cc}

    xs = [dev_f(around(x, k), zh, core) for k in range(4)]
    zs = [dev_f(x, around(zh, k), core) for k in range(4)]
    sib = dev_f(x, zh, 1 - core)
    ys = [{"space": zl * RING + around(y, k)} for k in range(4)]
    zsib = {"space": (1 - zl) * RING + y}

    partners = [zs[1], zs[3], xs[1], xs[3], ys[1], ys[3], sib, zsib]
    barrier = pltpu.get_barrier_semaphore()
    for other in partners:
        pl.semaphore_signal(barrier, inc=1, device_id=other, device_id_type=MESH)
    loads = []

    def load(src, dst):
        copy = pltpu.make_async_copy(src, dst, load_sems.at[len(loads)])
        copy.start()
        loads.append(copy)

    for h in range(heads):
        part = slice(h * HD, (h + 1) * HD)
        load(w_ref.at[:, part], wb.at[h, x, zh, core])
        load(k_ref.at[:, part], kv8.at[h, x, core, 0])
        load(v_ref.at[:, part], kv8.at[h, x, core, 1])
        load(q_ref.at[:, part], q4.at[h, zh])
        if h == 0:
            load(g_ref, g8.at[zl, y])
    for copy in loads:
        copy.wait()
    pl.semaphore_wait(barrier, len(partners))

    used = [0]
    pending = []

    def send(src, dst, device):
        n = used[0]
        used[0] += 1
        copy = pltpu.make_async_remote_copy(
            src_ref=src, dst_ref=dst, send_sem=send_sems.at[n], recv_sem=recv_sems.at[n],
            device_id=device, device_id_type=MESH)
        copy.start()
        pending.append(copy)
        return copy

    def gather(own, at, lo, hi, i, devs, forward=None):
        p, n, o = around(i, 1), around(i, 3), around(i, 2)
        first = [(send(src, dst, devs[1]), send(src, dst, devs[3])) for src, dst in own]
        fw = []
        if forward is not None:
            fw += [send(src, dst, forward) for src, dst in own]
        yield
        for c0, _ in first:
            c0.wait_recv()
        c2 = send(lo(n), lo(n), devs[1])
        if forward is not None:
            fw.append(send(at(n), at(n), forward))
        for _, c1 in first:
            c1.wait_recv()
        c3 = send(hi(p), hi(p), devs[3])
        if forward is not None:
            fw.append(send(at(p), at(p), forward))
        yield
        c2.wait_recv()
        c3.wait_recv()
        if forward is not None:
            fw.append(send(at(o), at(o), forward))
            yield
            for c in fw:
                c.wait_recv()

    def add_into(dst, landed):
        dst[...] = (dst[...].astype(F32) + landed[...].astype(F32)).astype(BF16)

    def scatter(blk, size, land, i, devs, out):
        h = size // 2
        p, n, o = around(i, 1), around(i, 3), around(i, 2)
        a0, b0 = land.at[0, 0:h], land.at[0, h:size]
        from_n, from_p = land.at[1], land.at[2]
        c0 = send(blk(o, 0, h), a0, devs[1])
        c1 = send(blk(o, h, size), b0, devs[3])
        c2 = send(blk(p, h, size), land.at[1, h:size], devs[1])
        c3 = send(blk(n, 0, h), land.at[2, 0:h], devs[3])
        yield
        c0.wait_recv()
        add_into(blk(p, 0, h), a0)
        c4 = send(blk(p, 0, h), land.at[1, 0:h], devs[1])
        c1.wait_recv()
        add_into(blk(n, h, size), b0)
        c5 = send(blk(n, h, size), land.at[2, h:size], devs[3])
        yield
        for c in (c2, c3, c4, c5):
            c.wait_recv()
        out(blk(i, 0, size)[...].astype(F32) + from_n[...].astype(F32) + from_p[...].astype(F32))

    def spread(src, land):
        copies = [send(src, land.at[zh], zs[k]) for k in (1, 3, 2)]
        yield
        for c in copies:
            c.wait_recv()

    def pump(*flows):
        for flow in flows:
            next(flow, None)

    def cols(h):
        return slice(h * HD, (h + 1) * HD)

    half = rows // 2
    hw = wcols // 2
    H = range(heads)

    def q_flow(h):
        own = [(q4.at[h, zh], q4.at[h, zh])]
        return gather(own, lambda j: q4.at[h, j], lambda j: q4.at[h, j, 0:half],
                      lambda j: q4.at[h, j, half:rows], zh, zs)

    def kv_flow(h):
        own = [(kv8.at[h, x, core], kv8.at[h, x, core])]
        return gather(own, lambda j: kv8.at[h, j, core], lambda j: kv8.at[h, j, core, 0],
                      lambda j: kv8.at[h, j, core, 1], x, xs, sib)

    def wz_flow(h):
        own = [(wb.at[h, x, zh, core], wb.at[h, x, zh, core])]
        return gather(own, lambda j: wb.at[h, x, j, core], lambda j: wb.at[h, x, j, core, 0:hw],
                      lambda j: wb.at[h, x, j, core, hw:wcols], zh, zs)

    def wx_flow(h):
        own = [(wb.at[h, x, :, core], wb.at[h, x, :, core])]
        return gather(own, lambda j: wb.at[h, j, :, core], lambda j: wb.at[h, j, 0:2, core],
                      lambda j: wb.at[h, j, 2:4, core], x, xs, sib)

    def g_flow():
        c = send(g8.at[zl, y], g8.at[zl, y], zsib)
        yield
        c.wait_recv()
        own = [(g8.at[:, y], g8.at[:, y])]
        yield from gather(own, lambda j: g8.at[:, j], lambda j: g8.at[0, j],
                          lambda j: g8.at[1, j], y, ys)

    def do_flow(h):
        own = [(da.at[h], do4.at[h, zh])]
        return gather(own, lambda j: do4.at[h, j], lambda j: do4.at[h, j, 0:half],
                      lambda j: do4.at[h, j, half:rows], zh, zs)

    def turn(h):
        qt[h] = q4[h].reshape(nq, HD).T
        for j in range(RING):
            kt[h, j] = kv8[h, j, :, 0].reshape(kc, HD).T
            vt[h, j] = kv8[h, j, :, 1].reshape(kc, HD).T

    tops, sums = {}, {}

    def logits_pass(h):
        def body(j, m8):
            sc = mm(kv8[h, j, :, 0].reshape(kc, HD), qt[h])
            s_buf[j] = sc
            return jnp.maximum(m8, jnp.max(sc.reshape(kc // 8, 8, nq), axis=0))
        m8 = lax.fori_loop(0, RING, body, jnp.full((8, nq), -jnp.inf, F32))
        tops[h] = jnp.max(m8, axis=0, keepdims=True)

    def probs_pass(h):
        m = tops[h]
        ot[h] = jnp.zeros((HD, nq), F32)

        def body(j, l8):
            pr = jnp.exp2((s_buf[j] - m) * c2)
            low = pr.astype(BF16)
            p_buf[h, j] = low
            ot[h] += mm(vt[h, j], low)
            return l8 + jnp.sum(pr.reshape(kc // 8, 8, nq), axis=0)
        l8 = lax.fori_loop(0, RING, body, jnp.zeros((8, nq), F32))
        sums[h] = jnp.sum(l8, axis=0, keepdims=True)
        l_out[h] = m * c2 + jnp.log2(sums[h])

    scales = {}

    def partial_out(h):
        ob[h] = (ot[h] / sums[h]).T.astype(BF16).reshape(RING, rows, HD)

    def weigh(h):
        l_in[h, zh] = l_out[h]
        ls = [l_in[h, around(zh, k)] for k in range(RING)]
        top = jnp.maximum(jnp.maximum(ls[0], ls[1]), jnp.maximum(ls[2], ls[3]))
        full = top + jnp.log2(sum(jnp.exp2(v - top) for v in ls))
        scales[h] = jnp.exp2(tops[h] * c2 - full)
        table = jnp.concatenate(
            [jnp.exp2(ls[k] - full) for k in (0, 3, 1)] + [jnp.zeros((5, nq), F32)], axis=0)
        wc[h] = table.T.reshape(RING, rows, 8)

    def o_flow(h):
        p, n, o = around(zh, 1), around(zh, 3), around(zh, 2)
        blk = ob.at[h]
        land = ol.at[h]
        lo, hi = slice(0, half), slice(half, rows)

        def w(j, part, k):
            return wc[h, j, part, k:k + 1]

        def wide(ref):
            return ref[...].astype(F32)
        c0 = send(blk.at[o, lo], land.at[0, lo], zs[1])
        c1 = send(blk.at[o, hi], land.at[0, hi], zs[3])
        c2_ = send(blk.at[p, hi], land.at[1, hi], zs[1])
        c3 = send(blk.at[n, lo], land.at[2, lo], zs[3])
        yield
        c0.wait_recv()
        mine = blk.at[p, lo]
        mine[...] = (wide(mine) * w(p, lo, 0) + wide(land.at[0, lo]) * w(p, lo, 1)).astype(BF16)
        c4 = send(mine, land.at[1, lo], zs[1])
        c1.wait_recv()
        mine = blk.at[n, hi]
        mine[...] = (wide(mine) * w(n, hi, 0) + wide(land.at[0, hi]) * w(n, hi, 2)).astype(BF16)
        c5 = send(mine, land.at[2, hi], zs[3])
        yield
        for c in (c2_, c3, c4, c5):
            c.wait_recv()
        at[h, lo] = (wide(blk.at[zh, lo]) * w(zh, lo, 0) + wide(land.at[1, lo])
                     + wide(land.at[2, lo]) * w(zh, lo, 2)).astype(BF16)
        at[h, hi] = (wide(blk.at[zh, hi]) * w(zh, hi, 0) + wide(land.at[1, hi]) * w(zh, hi, 1)
                     + wide(land.at[2, hi])).astype(BF16)

    def grad_attn(h):
        acc = jnp.zeros((rows, HD), F32)
        for t in range(PAIR * RING):
            block = wb[h, t // 2, 2 * (t % 2):2 * (t % 2) + 2].reshape(width, HD)
            acc = acc + mm(g8[t // RING, t % RING], block)
        low = acc.astype(BF16)
        da[h] = low
        do4[h, zh] = low

    def row_terms(h):
        scaled = do4[h].reshape(nq, HD).astype(F32).T * scales[h]
        u_out[h] = jnp.sum(scaled * ot[h], axis=0, keepdims=True)
        dsl[h] = scaled.astype(BF16)
        don[h] = scaled.T.astype(BF16)

    def backward(h):
        u_in[h, zh] = u_out[h]
        dl = (u_in[h, 0] + u_in[h, 1] + u_in[h, 2] + u_in[h, 3]) * scales[h]
        dqt[...] = jnp.zeros_like(dqt)

        def body(j, unused):
            dp = mm(kv8[h, j, :, 1].reshape(kc, HD), dsl[h])
            pr = p_buf[h, j]
            dlog = (pr.astype(F32) * (dp - dl)).astype(BF16)
            dkvb[h, :, j, 1] = mm(pr, don[h]).astype(BF16).reshape(CORES, rows, HD)
            dkvb[h, :, j, 0] = (factor * mm(dlog, q4[h].reshape(nq, HD))).astype(
                BF16).reshape(CORES, rows, HD)
            dqt[...] += mm(kt[h, j], dlog)
            return unused
        lax.fori_loop(0, RING, body, 0)
        dqb[h] = (factor * dqt[...]).T.astype(BF16).reshape(RING, rows, HD)

    def proj(h):
        for t in range(PAIR * RING):
            part = mm(gt[t], at[h])
            gpb[h, t // 2, 2 * (t % 2):2 * (t % 2) + 2] = part.astype(BF16).reshape(
                2, CORES, wcols, HD)

    def dkv_flow(h):
        c = send(dkvb.at[h, 1 - core], dkvc.at[h], sib)
        yield
        c.wait_recv()
        add_into(dkvb.at[h, core], dkvc.at[h])

        def write(value):
            dk_ref[:, cols(h)] = value[0].astype(BF16)
            dv_ref[:, cols(h)] = value[1].astype(BF16)
        yield from scatter(lambda j, lo, hi: dkvb.at[h, core, j, lo:hi], 2, dkvl.at[h], x, xs,
                           write)

    def dq_flow(h):
        def write(value):
            dq_ref[:, cols(h)] = value.astype(BF16)
        return scatter(lambda j, lo, hi: dqb.at[h, j, lo:hi], rows, dql.at[h], zh, zs, write)

    def gp_flow(h):
        c = send(gpb.at[h, :, :, 1 - core], gpc.at[h], sib)
        yield
        c.wait_recv()
        for j in range(RING):
            add_into(gpb.at[h, j, :, core], gpc.at[h, j])

        def keep(value):
            gpr[h] = value.astype(BF16)
        yield from scatter(lambda j, lo, hi: gpb.at[h, j, lo:hi, core], RING, gpx.at[h], x, xs,
                           keep)

        def final(value):
            gp_ref[:, cols(h)] = value
        yield from scatter(lambda j, lo, hi: gpr.at[h, j, lo:hi], wcols, gpz.at[h], zh, zs, final)

    QZ, KV, WZ = [q_flow(h) for h in H], [kv_flow(h) for h in H], [wz_flow(h) for h in H]
    WX, DZ, OZ = [wx_flow(h) for h in H], [do_flow(h) for h in H], [o_flow(h) for h in H]
    LX = [spread(l_out.at[h], l_in.at[h]) for h in H]
    UX = [spread(u_out.at[h], u_in.at[h]) for h in H]
    DK, DQ, GP = [dkv_flow(h) for h in H], [dq_flow(h) for h in H], [gp_flow(h) for h in H]
    G = g_flow()
    def turn_g():
        for t in range(PAIR * RING):
            gt[t] = g8[t // RING, t % RING].T

    steps = {"gt": turn_g}
    flows = {"G": g_flow()}
    for h in H:
        for name, make in (("Q", q_flow), ("K", kv_flow), ("W", wz_flow), ("X", wx_flow),
                           ("D", do_flow), ("O", o_flow), ("V", dkv_flow), ("E", dq_flow),
                           ("Y", gp_flow)):
            flows[name + str(h)] = make(h)
        flows["l" + str(h)] = spread(l_out.at[h], l_in.at[h])
        flows["u" + str(h)] = spread(u_out.at[h], u_in.at[h])
        for name, call in (("T", turn), ("L", logits_pass), ("P", probs_pass), ("N", partial_out), ("M", weigh),
                           ("A", grad_attn), ("R", row_terms), ("B", backward), ("J", proj)):
            steps[name + str(h)] = functools.partial(call, h)
    for name in ORDER:
        if name in steps:
            steps[name]()
        else:
            next(flows[name[:-1]], None)
    for flow in flows.values():
        assert next(flow, flow) is flow
    for c in pending:
        c.wait_send()
    assert used[0] <= nsem, used[0]


def keep(*refs):
    for src, dst in zip(refs[:4], refs[4:]):
        dst[...] = src[...]


def local(queries, keys, values, grad_out, proj_weight):
    rows, width = queries.shape
    heads = width // HD
    wcols = proj_weight.shape[1]
    nq, kc = RING * rows, CORES * rows
    nsem = 240

    def vm(*shape, dtype=BF16):
        return pltpu.VMEM(shape, dtype)

    scratch = [
        vm(heads, RING, rows, HD), vm(heads, RING, CORES, 2, rows, HD),
        vm(PAIR, RING, rows, width), vm(PAIR * RING, width, rows),
        vm(heads, RING, RING, CORES, wcols, HD),
        vm(heads, rows, HD), vm(heads, RING, rows, HD),
        vm(heads, HD, nq), vm(heads, RING, HD, kc), vm(heads, RING, HD, kc),
        vm(heads, nq, HD), vm(heads, HD, nq), vm(heads, rows, HD),
        vm(heads, RING, rows, 8, dtype=F32),
        vm(RING, kc, nq, dtype=F32), vm(heads, RING, kc, nq), vm(heads, HD, nq, dtype=F32),
        vm(heads, RING, 1, nq, dtype=F32), vm(heads, 1, nq, dtype=F32),
        vm(heads, 1, nq, dtype=F32), vm(heads, RING, 1, nq, dtype=F32),
        vm(heads, RING, rows, HD), vm(heads, 3, rows, HD),
        vm(HD, nq, dtype=F32), vm(heads, RING, rows, HD), vm(heads, 3, rows, HD),
        vm(heads, CORES, RING, 2, rows, HD), vm(heads, RING, 2, rows, HD),
        vm(heads, 3, 2, rows, HD),
        vm(heads, RING, RING, CORES, wcols, HD), vm(heads, RING, RING, wcols, HD),
        vm(heads, 3, RING, wcols, HD), vm(heads, 3, wcols, HD), vm(heads, RING, wcols, HD),
        pltpu.SemaphoreType.DMA((4 * heads + 1,)),
        pltpu.SemaphoreType.DMA((nsem,)), pltpu.SemaphoreType.DMA((nsem,)),
    ]
    vmem = pl.BlockSpec(memory_space=pltpu.VMEM)

    def body(*refs):
        kernel((rows, heads, wcols, nsem), *refs)

    like = jax.ShapeDtypeStruct((rows, width), BF16)
    dq, dk, dv, gp = pl.pallas_call(
        body,
        out_shape=(pltpu.VMEM((rows, width), BF16),) * 3 + (pltpu.VMEM((wcols, width), F32),),
        in_specs=[pl.BlockSpec(memory_space=pl.ANY)] * 5,
        out_specs=(vmem,) * 4,
        scratch_shapes=scratch,
        compiler_params=pltpu.CompilerParams(
            collective_id=0, has_side_effects=True, vmem_limit_bytes=60 * 1024 * 1024),
        name="fused",
    )(queries, keys, values, grad_out, proj_weight.T)
    dq, dk, dv, gp = pl.pallas_call(
        keep,
        out_shape=(like, like, like, jax.ShapeDtypeStruct((wcols, width), F32)),
        in_specs=[vmem] * 4,
        out_specs=(vmem,) * 4,
        name="keep",
    )(*(pltpu.with_memory_space_constraint(v, pltpu.VMEM) for v in (dq, dk, dv, gp)))
    return dq, dk, dv, gp.T


def solution(mesh):
    spec = P("frame", "space")
    return jax.shard_map(
        local, mesh=mesh, in_specs=(spec,) * 4 + (P("space", "frame"),),
        out_specs=(spec,) * 3 + (P("space", "frame"),), check_vma=False)
```

```python
import functools
import math

import jax
import jax.numpy as jnp
from jax import lax
from jax.experimental import pallas as pl
from jax.experimental.pallas import tpu as pltpu
from jax.sharding import PartitionSpec as P

HD = 128
MESH = pl.DeviceIdType.MESH
F32 = jnp.float32
BF16 = jnp.bfloat16
RING = 4
CORES = 2
PAIR = 2


ORDER = (
    "W01", "K11", "K01", "W11", "G1", "W02", "Q01", "K12", "K02", "W12", "G2", "W21", "K21",
    "Q11", "W03", "X01", "Q02", "W13", "K13", "Q21", "X11", "K03", "W22", "X02", "Q12", "K22",
    "K04", "G3", "K14", "Q03", "T0", "L0", "P0", "l01", "W23", "X21", "Q22", "X03", "N0", "O01",
    "K23", "Q13", "X12", "T1", "L1", "G4", "X04", "A0", "D01", "P1", "Q23", "l11", "X22", "l02",
    "M0", "O02", "N1", "K24", "X13", "O11", "T2", "L2", "gt", "D02", "X14", "A1", "X23", "D11",
    "P2", "O03", "J0", "l12", "l21", "N2", "M1", "Y01", "X24", "O12", "A2", "D21", "D03", "R0",
    "u01", "D12", "Y02", "O21", "O13", "J1", "Y11", "l22", "D22", "M2", "Y03", "D13", "R1", "u11",
    "Y12", "u02", "O22", "B0", "V01", "D23", "R2", "u21", "Y04", "E01", "Y13", "O23", "J2", "Y21",
    "u12", "B1", "V11", "Y22", "V02", "Y14", "u22", "E11", "B2", "Y23", "V21", "E02", "V12",
    "E21", "Y15", "V22", "Y24", "Y05", "V03", "E22", "E12", "V13", "V23", "Y25", "E23", "V14",
    "V24", "Y16", "Y06", "E03", "E13", "V04", "Y26",
)


def mm(a, b):
    return jnp.dot(a, b, preferred_element_type=F32)


def kernel(dims, q_ref, k_ref, v_ref, g_ref, w_ref, dq_ref, dk_ref, dv_ref, gp_ref, *scratch):
    rows, heads, wcols, nsem = dims
    (q4, kv8, g8, gt, wb, da, do4, qt, kt, vt, don, dsl, at, wc, s_buf, p_buf, ot, l_in, u_out, l_out, u_in,
     ob, ol, dqt, dqb, dql, dkvb, dkvc, dkvl, gpb, gpc, gpx, gpz, gpr,
     load_sems, send_sems, recv_sems) = scratch
    width = heads * HD
    nq = RING * rows
    kc = CORES * rows
    factor = 1.0 / math.sqrt(HD)
    c2 = factor * math.log2(math.e)

    f = lax.axis_index("frame")
    s = lax.axis_index("space")
    x, zh, core = f // 8, lax.rem(f // 2, 4), lax.rem(f, 2)
    zl, y = s // 4, lax.rem(s, 4)

    def around(i, k):
        return lax.rem(i + k, RING)

    def dev_f(xx, zz, cc):
        return {"frame": (xx * RING + zz) * CORES + cc}

    xs = [dev_f(around(x, k), zh, core) for k in range(4)]
    zs = [dev_f(x, around(zh, k), core) for k in range(4)]
    sib = dev_f(x, zh, 1 - core)
    ys = [{"space": zl * RING + around(y, k)} for k in range(4)]
    zsib = {"space": (1 - zl) * RING + y}

    partners = [zs[1], zs[3], xs[1], xs[3], ys[1], ys[3], sib, zsib]
    barrier = pltpu.get_barrier_semaphore()
    for other in partners:
        pl.semaphore_signal(barrier, inc=1, device_id=other, device_id_type=MESH)
    loads = []

    def load(src, dst):
        copy = pltpu.make_async_copy(src, dst, load_sems.at[len(loads)])
        copy.start()
        loads.append(copy)

    for h in range(heads):
        part = slice(h * HD, (h + 1) * HD)
        load(w_ref.at[:, part], wb.at[h, x, zh, core])
        load(k_ref.at[:, part], kv8.at[h, x, core, 0])
        load(v_ref.at[:, part], kv8.at[h, x, core, 1])
        load(q_ref.at[:, part], q4.at[h, zh])
        if h == 0:
            load(g_ref, g8.at[zl, y])
    for copy in loads:
        copy.wait()
    pl.semaphore_wait(barrier, len(partners))

    used = [0]
    pending = []

    def send(src, dst, device):
        n = used[0]
        used[0] += 1
        copy = pltpu.make_async_remote_copy(
            src_ref=src, dst_ref=dst, send_sem=send_sems.at[n], recv_sem=recv_sems.at[n],
            device_id=device, device_id_type=MESH)
        copy.start()
        pending.append(copy)
        return copy

    def gather(own, at, lo, hi, i, devs, forward=None):
        p, n, o = around(i, 1), around(i, 3), around(i, 2)
        first = [(send(src, dst, devs[1]), send(src, dst, devs[3])) for src, dst in own]
        fw = []
        if forward is not None:
            fw += [send(src, dst, forward) for src, dst in own]
        yield
        for c0, _ in first:
            c0.wait_recv()
        c2 = send(lo(n), lo(n), devs[1])
        if forward is not None:
            fw.append(send(at(n), at(n), forward))
        for _, c1 in first:
            c1.wait_recv()
        c3 = send(hi(p), hi(p), devs[3])
        if forward is not None:
            fw.append(send(at(p), at(p), forward))
        yield
        c2.wait_recv()
        c3.wait_recv()
        if forward is not None:
            fw.append(send(at(o), at(o), forward))
            yield
            for c in fw:
                c.wait_recv()

    def add_into(dst, landed):
        dst[...] = (dst[...].astype(F32) + landed[...].astype(F32)).astype(BF16)

    def scatter(blk, size, land, i, devs, out):
        h = size // 2
        p, n, o = around(i, 1), around(i, 3), around(i, 2)
        a0, b0 = land.at[0, 0:h], land.at[0, h:size]
        from_n, from_p = land.at[1], land.at[2]
        c0 = send(blk(o, 0, h), a0, devs[1])
        c1 = send(blk(o, h, size), b0, devs[3])
        c2 = send(blk(p, h, size), land.at[1, h:size], devs[1])
        c3 = send(blk(n, 0, h), land.at[2, 0:h], devs[3])
        yield
        c0.wait_recv()
        add_into(blk(p, 0, h), a0)
        c4 = send(blk(p, 0, h), land.at[1, 0:h], devs[1])
        c1.wait_recv()
        add_into(blk(n, h, size), b0)
        c5 = send(blk(n, h, size), land.at[2, h:size], devs[3])
        yield
        for c in (c2, c3, c4, c5):
            c.wait_recv()
        out(blk(i, 0, size)[...].astype(F32) + from_n[...].astype(F32) + from_p[...].astype(F32))

    def spread(src, land):
        copies = [send(src, land.at[zh], zs[k]) for k in (1, 3, 2)]
        yield
        for c in copies:
            c.wait_recv()

    def pump(*flows):
        for flow in flows:
            next(flow, None)

    def cols(h):
        return slice(h * HD, (h + 1) * HD)

    half = rows // 2
    hw = wcols // 2
    H = range(heads)

    def q_flow(h):
        own = [(q4.at[h, zh], q4.at[h, zh])]
        return gather(own, lambda j: q4.at[h, j], lambda j: q4.at[h, j, 0:half],
                      lambda j: q4.at[h, j, half:rows], zh, zs)

    def kv_flow(h):
        own = [(kv8.at[h, x, core], kv8.at[h, x, core])]
        return gather(own, lambda j: kv8.at[h, j, core], lambda j: kv8.at[h, j, core, 0],
                      lambda j: kv8.at[h, j, core, 1], x, xs, sib)

    def wz_flow(h):
        own = [(wb.at[h, x, zh, core], wb.at[h, x, zh, core])]
        return gather(own, lambda j: wb.at[h, x, j, core], lambda j: wb.at[h, x, j, core, 0:hw],
                      lambda j: wb.at[h, x, j, core, hw:wcols], zh, zs)

    def wx_flow(h):
        own = [(wb.at[h, x, :, core], wb.at[h, x, :, core])]
        return gather(own, lambda j: wb.at[h, j, :, core], lambda j: wb.at[h, j, 0:2, core],
                      lambda j: wb.at[h, j, 2:4, core], x, xs, sib)

    def g_flow():
        c = send(g8.at[zl, y], g8.at[zl, y], zsib)
        yield
        c.wait_recv()
        own = [(g8.at[:, y], g8.at[:, y])]
        yield from gather(own, lambda j: g8.at[:, j], lambda j: g8.at[0, j],
                          lambda j: g8.at[1, j], y, ys)

    def do_flow(h):
        own = [(da.at[h], do4.at[h, zh])]
        return gather(own, lambda j: do4.at[h, j], lambda j: do4.at[h, j, 0:half],
                      lambda j: do4.at[h, j, half:rows], zh, zs)

    def turn(h):
        qt[h] = q4[h].reshape(nq, HD).T
        for j in range(RING):
            kt[h, j] = kv8[h, j, :, 0].reshape(kc, HD).T
            vt[h, j] = kv8[h, j, :, 1].reshape(kc, HD).T

    tops, sums = {}, {}

    def logits_pass(h):
        def body(j, m8):
            sc = mm(kv8[h, j, :, 0].reshape(kc, HD), qt[h])
            s_buf[j] = sc
            return jnp.maximum(m8, jnp.max(sc.reshape(kc // 8, 8, nq), axis=0))
        m8 = lax.fori_loop(0, RING, body, jnp.full((8, nq), -jnp.inf, F32), unroll=True)
        tops[h] = jnp.max(m8, axis=0, keepdims=True)

    def probs_pass(h):
        m = tops[h]
        ot[h] = jnp.zeros((HD, nq), F32)

        def body(j, l8):
            pr = jnp.exp2((s_buf[j] - m) * c2)
            low = pr.astype(BF16)
            p_buf[h, j] = low
            ot[h] += mm(vt[h, j], low)
            return l8 + jnp.sum(pr.reshape(kc // 8, 8, nq), axis=0)
        l8 = lax.fori_loop(0, RING, body, jnp.zeros((8, nq), F32), unroll=True)
        sums[h] = jnp.sum(l8, axis=0, keepdims=True)
        l_out[h] = m * c2 + jnp.log2(sums[h])

    scales = {}

    def partial_out(h):
        ob[h] = (ot[h] / sums[h]).T.astype(BF16).reshape(RING, rows, HD)

    def weigh(h):
        l_in[h, zh] = l_out[h]
        ls = [l_in[h, around(zh, k)] for k in range(RING)]
        top = jnp.maximum(jnp.maximum(ls[0], ls[1]), jnp.maximum(ls[2], ls[3]))
        full = top + jnp.log2(sum(jnp.exp2(v - top) for v in ls))
        scales[h] = jnp.exp2(tops[h] * c2 - full)
        table = jnp.concatenate(
            [jnp.exp2(ls[k] - full) for k in (0, 3, 1)] + [jnp.zeros((5, nq), F32)], axis=0)
        wc[h] = table.T.reshape(RING, rows, 8)

    def o_flow(h):
        p, n, o = around(zh, 1), around(zh, 3), around(zh, 2)
        blk = ob.at[h]
        land = ol.at[h]
        lo, hi = slice(0, half), slice(half, rows)

        def w(j, part, k):
            return wc[h, j, part, k:k + 1]

        def wide(ref):
            return ref[...].astype(F32)
        c0 = send(blk.at[o, lo], land.at[0, lo], zs[1])
        c1 = send(blk.at[o, hi], land.at[0, hi], zs[3])
        c2_ = send(blk.at[p, hi], land.at[1, hi], zs[1])
        c3 = send(blk.at[n, lo], land.at[2, lo], zs[3])
        yield
        c0.wait_recv()
        mine = blk.at[p, lo]
        mine[...] = (wide(mine) * w(p, lo, 0) + wide(land.at[0, lo]) * w(p, lo, 1)).astype(BF16)
        c4 = send(mine, land.at[1, lo], zs[1])
        c1.wait_recv()
        mine = blk.at[n, hi]
        mine[...] = (wide(mine) * w(n, hi, 0) + wide(land.at[0, hi]) * w(n, hi, 2)).astype(BF16)
        c5 = send(mine, land.at[2, hi], zs[3])
        yield
        for c in (c2_, c3, c4, c5):
            c.wait_recv()
        at[h, lo] = (wide(blk.at[zh, lo]) * w(zh, lo, 0) + wide(land.at[1, lo])
                     + wide(land.at[2, lo]) * w(zh, lo, 2)).astype(BF16)
        at[h, hi] = (wide(blk.at[zh, hi]) * w(zh, hi, 0) + wide(land.at[1, hi]) * w(zh, hi, 1)
                     + wide(land.at[2, hi])).astype(BF16)

    def grad_attn(h):
        acc = jnp.zeros((rows, HD), F32)
        for t in range(PAIR * RING):
            block = wb[h, t // 2, 2 * (t % 2):2 * (t % 2) + 2].reshape(width, HD)
            acc = acc + mm(g8[t // RING, t % RING], block)
        low = acc.astype(BF16)
        da[h] = low
        do4[h, zh] = low

    def row_terms(h):
        scaled = do4[h].reshape(nq, HD).astype(F32).T * scales[h]
        u_out[h] = jnp.sum(scaled * ot[h], axis=0, keepdims=True)
        dsl[h] = scaled.astype(BF16)
        don[h] = scaled.T.astype(BF16)

    def backward(h):
        u_in[h, zh] = u_out[h]
        dl = (u_in[h, 0] + u_in[h, 1] + u_in[h, 2] + u_in[h, 3]) * scales[h]
        dqt[...] = jnp.zeros_like(dqt)

        def body(j, unused):
            dp = mm(kv8[h, j, :, 1].reshape(kc, HD), dsl[h])
            pr = p_buf[h, j]
            dlog = (pr.astype(F32) * (dp - dl)).astype(BF16)
            dkvb[h, :, j, 1] = mm(pr, don[h]).astype(BF16).reshape(CORES, rows, HD)
            dkvb[h, :, j, 0] = (factor * mm(dlog, q4[h].reshape(nq, HD))).astype(
                BF16).reshape(CORES, rows, HD)
            dqt[...] += mm(kt[h, j], dlog)
            return unused
        lax.fori_loop(0, RING, body, 0, unroll=True)
        dqb[h] = (factor * dqt[...]).T.astype(BF16).reshape(RING, rows, HD)

    def proj(h):
        for t in range(PAIR * RING):
            part = mm(gt[t], at[h])
            gpb[h, t // 2, 2 * (t % 2):2 * (t % 2) + 2] = part.astype(BF16).reshape(
                2, CORES, wcols, HD)

    def dkv_flow(h):
        c = send(dkvb.at[h, 1 - core], dkvc.at[h], sib)
        yield
        c.wait_recv()
        add_into(dkvb.at[h, core], dkvc.at[h])

        def write(value):
            dk_ref[:, cols(h)] = value[0].astype(BF16)
            dv_ref[:, cols(h)] = value[1].astype(BF16)
        yield from scatter(lambda j, lo, hi: dkvb.at[h, core, j, lo:hi], 2, dkvl.at[h], x, xs,
                           write)

    def dq_flow(h):
        def write(value):
            dq_ref[:, cols(h)] = value.astype(BF16)
        return scatter(lambda j, lo, hi: dqb.at[h, j, lo:hi], rows, dql.at[h], zh, zs, write)

    def gp_flow(h):
        c = send(gpb.at[h, :, :, 1 - core], gpc.at[h], sib)
        yield
        c.wait_recv()
        for j in range(RING):
            add_into(gpb.at[h, j, :, core], gpc.at[h, j])

        def keep(value):
            gpr[h] = value.astype(BF16)
        yield from scatter(lambda j, lo, hi: gpb.at[h, j, lo:hi, core], RING, gpx.at[h], x, xs,
                           keep)

        def final(value):
            gp_ref[:, cols(h)] = value
        yield from scatter(lambda j, lo, hi: gpr.at[h, j, lo:hi], wcols, gpz.at[h], zh, zs, final)

    QZ, KV, WZ = [q_flow(h) for h in H], [kv_flow(h) for h in H], [wz_flow(h) for h in H]
    WX, DZ, OZ = [wx_flow(h) for h in H], [do_flow(h) for h in H], [o_flow(h) for h in H]
    LX = [spread(l_out.at[h], l_in.at[h]) for h in H]
    UX = [spread(u_out.at[h], u_in.at[h]) for h in H]
    DK, DQ, GP = [dkv_flow(h) for h in H], [dq_flow(h) for h in H], [gp_flow(h) for h in H]
    G = g_flow()
    def turn_g():
        for t in range(PAIR * RING):
            gt[t] = g8[t // RING, t % RING].T

    steps = {"gt": turn_g}
    flows = {"G": g_flow()}
    for h in H:
        for name, make in (("Q", q_flow), ("K", kv_flow), ("W", wz_flow), ("X", wx_flow),
                           ("D", do_flow), ("O", o_flow), ("V", dkv_flow), ("E", dq_flow),
                           ("Y", gp_flow)):
            flows[name + str(h)] = make(h)
        flows["l" + str(h)] = spread(l_out.at[h], l_in.at[h])
        flows["u" + str(h)] = spread(u_out.at[h], u_in.at[h])
        for name, call in (("T", turn), ("L", logits_pass), ("P", probs_pass), ("N", partial_out), ("M", weigh),
                           ("A", grad_attn), ("R", row_terms), ("B", backward), ("J", proj)):
            steps[name + str(h)] = functools.partial(call, h)
    for name in ORDER:
        if name in steps:
            steps[name]()
        else:
            next(flows[name[:-1]], None)
    for flow in flows.values():
        assert next(flow, flow) is flow
    for c in pending:
        c.wait_send()
    assert used[0] <= nsem, used[0]


def keep(*refs):
    for src, dst in zip(refs[:4], refs[4:]):
        dst[...] = src[...]


def local(queries, keys, values, grad_out, proj_weight):
    rows, width = queries.shape
    heads = width // HD
    wcols = proj_weight.shape[1]
    nq, kc = RING * rows, CORES * rows
    nsem = 240

    def vm(*shape, dtype=BF16):
        return pltpu.VMEM(shape, dtype)

    scratch = [
        vm(heads, RING, rows, HD), vm(heads, RING, CORES, 2, rows, HD),
        vm(PAIR, RING, rows, width), vm(PAIR * RING, width, rows),
        vm(heads, RING, RING, CORES, wcols, HD),
        vm(heads, rows, HD), vm(heads, RING, rows, HD),
        vm(heads, HD, nq), vm(heads, RING, HD, kc), vm(heads, RING, HD, kc),
        vm(heads, nq, HD), vm(heads, HD, nq), vm(heads, rows, HD),
        vm(heads, RING, rows, 8, dtype=F32),
        vm(RING, kc, nq, dtype=F32), vm(heads, RING, kc, nq), vm(heads, HD, nq, dtype=F32),
        vm(heads, RING, 1, nq, dtype=F32), vm(heads, 1, nq, dtype=F32),
        vm(heads, 1, nq, dtype=F32), vm(heads, RING, 1, nq, dtype=F32),
        vm(heads, RING, rows, HD), vm(heads, 3, rows, HD),
        vm(HD, nq, dtype=F32), vm(heads, RING, rows, HD), vm(heads, 3, rows, HD),
        vm(heads, CORES, RING, 2, rows, HD), vm(heads, RING, 2, rows, HD),
        vm(heads, 3, 2, rows, HD),
        vm(heads, RING, RING, CORES, wcols, HD), vm(heads, RING, RING, wcols, HD),
        vm(heads, 3, RING, wcols, HD), vm(heads, 3, wcols, HD), vm(heads, RING, wcols, HD),
        pltpu.SemaphoreType.DMA((4 * heads + 1,)),
        pltpu.SemaphoreType.DMA((nsem,)), pltpu.SemaphoreType.DMA((nsem,)),
    ]
    vmem = pl.BlockSpec(memory_space=pltpu.VMEM)

    def body(*refs):
        kernel((rows, heads, wcols, nsem), *refs)

    like = jax.ShapeDtypeStruct((rows, width), BF16)
    dq, dk, dv, gp = pl.pallas_call(
        body,
        out_shape=(pltpu.VMEM((rows, width), BF16),) * 3 + (pltpu.VMEM((wcols, width), F32),),
        in_specs=[pl.BlockSpec(memory_space=pl.ANY)] * 5,
        out_specs=(vmem,) * 4,
        scratch_shapes=scratch,
        compiler_params=pltpu.CompilerParams(
            collective_id=0, has_side_effects=True, vmem_limit_bytes=60 * 1024 * 1024),
        name="fused",
    )(queries, keys, values, grad_out, proj_weight.T)
    dq, dk, dv, gp = pl.pallas_call(
        keep,
        out_shape=(like, like, like, jax.ShapeDtypeStruct((wcols, width), F32)),
        in_specs=[vmem] * 4,
        out_specs=(vmem,) * 4,
        name="keep",
    )(*(pltpu.with_memory_space_constraint(v, pltpu.VMEM) for v in (dq, dk, dv, gp)))
    return dq, dk, dv, gp.T


def solution(mesh):
    spec = P("frame", "space")
    return jax.shard_map(
        local, mesh=mesh, in_specs=(spec,) * 4 + (P("space", "frame"),),
        out_specs=(spec,) * 3 + (P("space", "frame"),), check_vma=False)
```

```python
import functools
import math

import jax
import jax.numpy as jnp
from jax import lax
from jax.experimental import pallas as pl
from jax.experimental.pallas import tpu as pltpu
from jax.sharding import PartitionSpec as P

HD = 128
MESH = pl.DeviceIdType.MESH
F32 = jnp.float32
BF16 = jnp.bfloat16
RING = 4
CORES = 2
PAIR = 2


ORDER = (
    "W01", "K11", "W11", "K01", "G1", "W02", "Q01", "K21", "W12", "K02", "W21", "G2", "K12",
    "Q11", "W03", "X01", "Q02", "Q21", "W13", "K03", "X11", "K13", "W22", "K04", "Q12", "X02",
    "K14", "K22", "Q03", "T0", "G3", "L0", "P0", "X12", "N0", "l01", "W23", "O01", "X21", "Q22",
    "X03", "Q13", "T1", "L1", "P1", "N1", "l11", "O11", "K23", "X13", "X04", "G4", "A0", "D01",
    "l02", "X22", "K24", "X14", "Q23", "M0", "A1", "O02", "D11", "T2", "L2", "l12", "P2", "M1",
    "l21", "O12", "X23", "N2", "D02", "gt", "O21", "O03", "X24", "J0", "Y01", "A2", "D21", "O13",
    "D12", "J1", "D03", "l22", "R0", "Y11", "M2", "u01", "O22", "Y02", "D22", "Y12", "D13", "R1",
    "u11", "O23", "J2", "Y21", "Y03", "u02", "B0", "V01", "Y13", "D23", "R2", "u21", "E01", "Y22",
    "u12", "B1", "V11", "E11", "Y04", "Y14", "Y23", "u22", "B2", "V21", "V12", "E21", "V02",
    "Y24", "Y05", "V22", "E02", "E12", "V13", "Y15", "V03", "E22", "Y25", "V23", "E13", "Y06",
    "E03", "V14", "V04", "Y16", "E23", "V24", "Y26",
)


def mm(a, b):
    return jnp.dot(a, b, preferred_element_type=F32)


def kernel(dims, q_ref, k_ref, v_ref, g_ref, w_ref, dq_ref, dk_ref, dv_ref, gp_ref, *scratch):
    rows, heads, wcols, nsem = dims
    (q4, kv8, g8, gt, wb, da, do4, qt, kt, vt, don, dsl, at, wc, s_buf, p_buf, ot, l_in, u_out, l_out, u_in,
     ob, ol, dqt, dqb, dql, dkvb, dkvc, dkvl, gpb, gpc, gpx, gpz, gpr,
     load_sems, send_sems, recv_sems) = scratch
    width = heads * HD
    nq = RING * rows
    kc = CORES * rows
    factor = 1.0 / math.sqrt(HD)
    c2 = factor * math.log2(math.e)

    f = lax.axis_index("frame")
    s = lax.axis_index("space")
    x, zh, core = f // 8, lax.rem(f // 2, 4), lax.rem(f, 2)
    zl, y = s // 4, lax.rem(s, 4)

    def around(i, k):
        return lax.rem(i + k, RING)

    def dev_f(xx, zz, cc):
        return {"frame": (xx * RING + zz) * CORES + cc}

    xs = [dev_f(around(x, k), zh, core) for k in range(4)]
    zs = [dev_f(x, around(zh, k), core) for k in range(4)]
    sib = dev_f(x, zh, 1 - core)
    ys = [{"space": zl * RING + around(y, k)} for k in range(4)]
    zsib = {"space": (1 - zl) * RING + y}

    partners = [zs[1], zs[3], xs[1], xs[3], ys[1], ys[3], sib, zsib]
    barrier = pltpu.get_barrier_semaphore()
    for other in partners:
        pl.semaphore_signal(barrier, inc=1, device_id=other, device_id_type=MESH)
    loads = []

    def load(src, dst):
        copy = pltpu.make_async_copy(src, dst, load_sems.at[len(loads)])
        copy.start()
        loads.append(copy)

    for h in range(heads):
        part = slice(h * HD, (h + 1) * HD)
        load(w_ref.at[:, part], wb.at[h, x, zh, core])
        load(k_ref.at[:, part], kv8.at[h, x, core, 0])
        load(v_ref.at[:, part], kv8.at[h, x, core, 1])
        load(q_ref.at[:, part], q4.at[h, zh])
        if h == 0:
            load(g_ref, g8.at[zl, y])
    for copy in loads:
        copy.wait()
    pl.semaphore_wait(barrier, len(partners))

    used = [0]
    pending = []

    def send(src, dst, device):
        n = used[0]
        used[0] += 1
        copy = pltpu.make_async_remote_copy(
            src_ref=src, dst_ref=dst, send_sem=send_sems.at[n], recv_sem=recv_sems.at[n],
            device_id=device, device_id_type=MESH)
        copy.start()
        pending.append(copy)
        return copy

    def gather(own, at, lo, hi, i, devs, forward=None):
        p, n, o = around(i, 1), around(i, 3), around(i, 2)
        first = [(send(src, dst, devs[1]), send(src, dst, devs[3])) for src, dst in own]
        fw = []
        if forward is not None:
            fw += [send(src, dst, forward) for src, dst in own]
        yield
        for c0, _ in first:
            c0.wait_recv()
        c2 = send(lo(n), lo(n), devs[1])
        if forward is not None:
            fw.append(send(at(n), at(n), forward))
        for _, c1 in first:
            c1.wait_recv()
        c3 = send(hi(p), hi(p), devs[3])
        if forward is not None:
            fw.append(send(at(p), at(p), forward))
        yield
        c2.wait_recv()
        c3.wait_recv()
        if forward is not None:
            fw.append(send(at(o), at(o), forward))
            yield
            for c in fw:
                c.wait_recv()

    def add_into(dst, landed):
        dst[...] = (dst[...].astype(F32) + landed[...].astype(F32)).astype(BF16)

    def scatter(blk, size, land, i, devs, out):
        h = size // 2
        p, n, o = around(i, 1), around(i, 3), around(i, 2)
        a0, b0 = land.at[0, 0:h], land.at[0, h:size]
        from_n, from_p = land.at[1], land.at[2]
        c0 = send(blk(o, 0, h), a0, devs[1])
        c1 = send(blk(o, h, size), b0, devs[3])
        c2 = send(blk(p, h, size), land.at[1, h:size], devs[1])
        c3 = send(blk(n, 0, h), land.at[2, 0:h], devs[3])
        yield
        c0.wait_recv()
        add_into(blk(p, 0, h), a0)
        c4 = send(blk(p, 0, h), land.at[1, 0:h], devs[1])
        c1.wait_recv()
        add_into(blk(n, h, size), b0)
        c5 = send(blk(n, h, size), land.at[2, h:size], devs[3])
        yield
        for c in (c2, c3, c4, c5):
            c.wait_recv()
        out(blk(i, 0, size)[...].astype(F32) + from_n[...].astype(F32) + from_p[...].astype(F32))

    def spread(src, land):
        copies = [send(src, land.at[zh], zs[k]) for k in (1, 3, 2)]
        yield
        for c in copies:
            c.wait_recv()

    def pump(*flows):
        for flow in flows:
            next(flow, None)

    def cols(h):
        return slice(h * HD, (h + 1) * HD)

    half = rows // 2
    hw = wcols // 2
    H = range(heads)

    def q_flow(h):
        own = [(q4.at[h, zh], q4.at[h, zh])]
        return gather(own, lambda j: q4.at[h, j], lambda j: q4.at[h, j, 0:half],
                      lambda j: q4.at[h, j, half:rows], zh, zs)

    def kv_flow(h):
        own = [(kv8.at[h, x, core], kv8.at[h, x, core])]
        return gather(own, lambda j: kv8.at[h, j, core], lambda j: kv8.at[h, j, core, 0],
                      lambda j: kv8.at[h, j, core, 1], x, xs, sib)

    def wz_flow(h):
        own = [(wb.at[h, x, zh, core], wb.at[h, x, zh, core])]
        return gather(own, lambda j: wb.at[h, x, j, core], lambda j: wb.at[h, x, j, core, 0:hw],
                      lambda j: wb.at[h, x, j, core, hw:wcols], zh, zs)

    def wx_flow(h):
        own = [(wb.at[h, x, :, core], wb.at[h, x, :, core])]
        return gather(own, lambda j: wb.at[h, j, :, core], lambda j: wb.at[h, j, 0:2, core],
                      lambda j: wb.at[h, j, 2:4, core], x, xs, sib)

    def g_flow():
        c = send(g8.at[zl, y], g8.at[zl, y], zsib)
        yield
        c.wait_recv()
        own = [(g8.at[:, y], g8.at[:, y])]
        yield from gather(own, lambda j: g8.at[:, j], lambda j: g8.at[0, j],
                          lambda j: g8.at[1, j], y, ys)

    def do_flow(h):
        own = [(da.at[h], do4.at[h, zh])]
        return gather(own, lambda j: do4.at[h, j], lambda j: do4.at[h, j, 0:half],
                      lambda j: do4.at[h, j, half:rows], zh, zs)

    def turn(h):
        qt[h] = q4[h].reshape(nq, HD).T
        for j in range(RING):
            kt[h, j] = kv8[h, j, :, 0].reshape(kc, HD).T
            vt[h, j] = kv8[h, j, :, 1].reshape(kc, HD).T

    tops, sums = {}, {}

    def logits_pass(h):
        def body(j, m8):
            sc = mm(kv8[h, j, :, 0].reshape(kc, HD), qt[h])
            s_buf[j] = sc
            return jnp.maximum(m8, jnp.max(sc.reshape(kc // 8, 8, nq), axis=0))
        m8 = lax.fori_loop(0, RING, body, jnp.full((8, nq), -jnp.inf, F32), unroll=True)
        tops[h] = jnp.max(m8, axis=0, keepdims=True)

    def probs_pass(h):
        m = tops[h]
        ot[h] = jnp.zeros((HD, nq), F32)

        def body(j, l8):
            pr = jnp.exp2((s_buf[j] - m) * c2)
            low = pr.astype(BF16)
            p_buf[h, j] = low
            ot[h] += mm(vt[h, j], low)
            return l8 + jnp.sum(pr.reshape(kc // 8, 8, nq), axis=0)
        l8 = lax.fori_loop(0, RING, body, jnp.zeros((8, nq), F32), unroll=True)
        sums[h] = jnp.sum(l8, axis=0, keepdims=True)
        l_out[h] = m * c2 + jnp.log2(sums[h])

    scales = {}

    def partial_out(h):
        ob[h] = (ot[h] / sums[h]).T.astype(BF16).reshape(RING, rows, HD)

    def weigh(h):
        l_in[h, zh] = l_out[h]
        ls = [l_in[h, around(zh, k)] for k in range(RING)]
        top = jnp.maximum(jnp.maximum(ls[0], ls[1]), jnp.maximum(ls[2], ls[3]))
        full = top + jnp.log2(sum(jnp.exp2(v - top) for v in ls))
        scales[h] = jnp.exp2(tops[h] * c2 - full)
        table = jnp.concatenate(
            [jnp.exp2(ls[k] - full) for k in (0, 3, 1)] + [jnp.zeros((5, nq), F32)], axis=0)
        wc[h] = table.T.reshape(RING, rows, 8)

    def o_flow(h):
        p, n, o = around(zh, 1), around(zh, 3), around(zh, 2)
        blk = ob.at[h]
        land = ol.at[h]
        lo, hi = slice(0, half), slice(half, rows)

        def w(j, part, k):
            return wc[h, j, part, k:k + 1]

        def wide(ref):
            return ref[...].astype(F32)
        c0 = send(blk.at[o, lo], land.at[0, lo], zs[1])
        c1 = send(blk.at[o, hi], land.at[0, hi], zs[3])
        c2_ = send(blk.at[p, hi], land.at[1, hi], zs[1])
        c3 = send(blk.at[n, lo], land.at[2, lo], zs[3])
        yield
        c0.wait_recv()
        mine = blk.at[p, lo]
        mine[...] = (wide(mine) * w(p, lo, 0) + wide(land.at[0, lo]) * w(p, lo, 1)).astype(BF16)
        c4 = send(mine, land.at[1, lo], zs[1])
        c1.wait_recv()
        mine = blk.at[n, hi]
        mine[...] = (wide(mine) * w(n, hi, 0) + wide(land.at[0, hi]) * w(n, hi, 2)).astype(BF16)
        c5 = send(mine, land.at[2, hi], zs[3])
        yield
        for c in (c2_, c3, c4, c5):
            c.wait_recv()
        at[h, lo] = (wide(blk.at[zh, lo]) * w(zh, lo, 0) + wide(land.at[1, lo])
                     + wide(land.at[2, lo]) * w(zh, lo, 2)).astype(BF16)
        at[h, hi] = (wide(blk.at[zh, hi]) * w(zh, hi, 0) + wide(land.at[1, hi]) * w(zh, hi, 1)
                     + wide(land.at[2, hi])).astype(BF16)

    def grad_attn(h):
        acc = jnp.zeros((rows, HD), F32)
        for t in range(PAIR * RING):
            block = wb[h, t // 2, 2 * (t % 2):2 * (t % 2) + 2].reshape(width, HD)
            acc = acc + mm(g8[t // RING, t % RING], block)
        low = acc.astype(BF16)
        da[h] = low
        do4[h, zh] = low

    def row_terms(h):
        scaled = do4[h].reshape(nq, HD).astype(F32).T * scales[h]
        u_out[h] = jnp.sum(scaled * ot[h], axis=0, keepdims=True)
        dsl[h] = scaled.astype(BF16)
        don[h] = scaled.T.astype(BF16)

    def backward(h):
        u_in[h, zh] = u_out[h]
        dl = (u_in[h, 0] + u_in[h, 1] + u_in[h, 2] + u_in[h, 3]) * scales[h]
        dqt[...] = jnp.zeros_like(dqt)

        def body(j, unused):
            dp = mm(kv8[h, j, :, 1].reshape(kc, HD), dsl[h])
            pr = p_buf[h, j]
            dlog = (pr.astype(F32) * (dp - dl)).astype(BF16)
            dkvb[h, :, j, 1] = mm(pr, don[h]).astype(BF16).reshape(CORES, rows, HD)
            dkvb[h, :, j, 0] = (factor * mm(dlog, q4[h].reshape(nq, HD))).astype(
                BF16).reshape(CORES, rows, HD)
            dqt[...] += mm(kt[h, j], dlog)
            return unused
        lax.fori_loop(0, RING, body, 0, unroll=True)
        dqb[h] = (factor * dqt[...]).T.astype(BF16).reshape(RING, rows, HD)

    def proj(h):
        for t in range(PAIR * RING):
            part = mm(gt[t], at[h])
            gpb[h, t // 2, 2 * (t % 2):2 * (t % 2) + 2] = part.astype(BF16).reshape(
                2, CORES, wcols, HD)

    def dkv_flow(h):
        c = send(dkvb.at[h, 1 - core], dkvc.at[h], sib)
        yield
        c.wait_recv()
        add_into(dkvb.at[h, core], dkvc.at[h])

        def write(value):
            dk_ref[:, cols(h)] = value[0].astype(BF16)
            dv_ref[:, cols(h)] = value[1].astype(BF16)
        yield from scatter(lambda j, lo, hi: dkvb.at[h, core, j, lo:hi], 2, dkvl.at[h], x, xs,
                           write)

    def dq_flow(h):
        def write(value):
            dq_ref[:, cols(h)] = value.astype(BF16)
        return scatter(lambda j, lo, hi: dqb.at[h, j, lo:hi], rows, dql.at[h], zh, zs, write)

    def gp_flow(h):
        c = send(gpb.at[h, :, :, 1 - core], gpc.at[h], sib)
        yield
        c.wait_recv()
        for j in range(RING):
            add_into(gpb.at[h, j, :, core], gpc.at[h, j])

        def keep(value):
            gpr[h] = value.astype(BF16)
        yield from scatter(lambda j, lo, hi: gpb.at[h, j, lo:hi, core], RING, gpx.at[h], x, xs,
                           keep)

        def final(value):
            gp_ref[:, cols(h)] = value
        yield from scatter(lambda j, lo, hi: gpr.at[h, j, lo:hi], wcols, gpz.at[h], zh, zs, final)

    QZ, KV, WZ = [q_flow(h) for h in H], [kv_flow(h) for h in H], [wz_flow(h) for h in H]
    WX, DZ, OZ = [wx_flow(h) for h in H], [do_flow(h) for h in H], [o_flow(h) for h in H]
    LX = [spread(l_out.at[h], l_in.at[h]) for h in H]
    UX = [spread(u_out.at[h], u_in.at[h]) for h in H]
    DK, DQ, GP = [dkv_flow(h) for h in H], [dq_flow(h) for h in H], [gp_flow(h) for h in H]
    G = g_flow()
    def turn_g():
        for t in range(PAIR * RING):
            gt[t] = g8[t // RING, t % RING].T

    steps = {"gt": turn_g}
    flows = {"G": g_flow()}
    for h in H:
        for name, make in (("Q", q_flow), ("K", kv_flow), ("W", wz_flow), ("X", wx_flow),
                           ("D", do_flow), ("O", o_flow), ("V", dkv_flow), ("E", dq_flow),
                           ("Y", gp_flow)):
            flows[name + str(h)] = make(h)
        flows["l" + str(h)] = spread(l_out.at[h], l_in.at[h])
        flows["u" + str(h)] = spread(u_out.at[h], u_in.at[h])
        for name, call in (("T", turn), ("L", logits_pass), ("P", probs_pass), ("N", partial_out), ("M", weigh),
                           ("A", grad_attn), ("R", row_terms), ("B", backward), ("J", proj)):
            steps[name + str(h)] = functools.partial(call, h)
    for name in ORDER:
        if name in steps:
            steps[name]()
        else:
            next(flows[name[:-1]], None)
    for flow in flows.values():
        assert next(flow, flow) is flow
    for c in pending:
        c.wait_send()
    assert used[0] <= nsem, used[0]


def keep(*refs):
    for src, dst in zip(refs[:4], refs[4:]):
        dst[...] = src[...]


def local(queries, keys, values, grad_out, proj_weight):
    rows, width = queries.shape
    heads = width // HD
    wcols = proj_weight.shape[1]
    nq, kc = RING * rows, CORES * rows
    nsem = 240

    def vm(*shape, dtype=BF16):
        return pltpu.VMEM(shape, dtype)

    scratch = [
        vm(heads, RING, rows, HD), vm(heads, RING, CORES, 2, rows, HD),
        vm(PAIR, RING, rows, width), vm(PAIR * RING, width, rows),
        vm(heads, RING, RING, CORES, wcols, HD),
        vm(heads, rows, HD), vm(heads, RING, rows, HD),
        vm(heads, HD, nq), vm(heads, RING, HD, kc), vm(heads, RING, HD, kc),
        vm(heads, nq, HD), vm(heads, HD, nq), vm(heads, rows, HD),
        vm(heads, RING, rows, 8, dtype=F32),
        vm(RING, kc, nq, dtype=F32), vm(heads, RING, kc, nq), vm(heads, HD, nq, dtype=F32),
        vm(heads, RING, 1, nq, dtype=F32), vm(heads, 1, nq, dtype=F32),
        vm(heads, 1, nq, dtype=F32), vm(heads, RING, 1, nq, dtype=F32),
        vm(heads, RING, rows, HD), vm(heads, 3, rows, HD),
        vm(HD, nq, dtype=F32), vm(heads, RING, rows, HD), vm(heads, 3, rows, HD),
        vm(heads, CORES, RING, 2, rows, HD), vm(heads, RING, 2, rows, HD),
        vm(heads, 3, 2, rows, HD),
        vm(heads, RING, RING, CORES, wcols, HD), vm(heads, RING, RING, wcols, HD),
        vm(heads, 3, RING, wcols, HD), vm(heads, 3, wcols, HD), vm(heads, RING, wcols, HD),
        pltpu.SemaphoreType.DMA((4 * heads + 1,)),
        pltpu.SemaphoreType.DMA((nsem,)), pltpu.SemaphoreType.DMA((nsem,)),
    ]
    vmem = pl.BlockSpec(memory_space=pltpu.VMEM)

    def body(*refs):
        kernel((rows, heads, wcols, nsem), *refs)

    like = jax.ShapeDtypeStruct((rows, width), BF16)
    dq, dk, dv, gp = pl.pallas_call(
        body,
        out_shape=(pltpu.VMEM((rows, width), BF16),) * 3 + (pltpu.VMEM((wcols, width), F32),),
        in_specs=[pl.BlockSpec(memory_space=pl.ANY)] * 5,
        out_specs=(vmem,) * 4,
        scratch_shapes=scratch,
        compiler_params=pltpu.CompilerParams(
            collective_id=0, has_side_effects=True, vmem_limit_bytes=60 * 1024 * 1024),
        name="fused",
    )(queries, keys, values, grad_out, proj_weight.T)
    dq, dk, dv, gp = pl.pallas_call(
        keep,
        out_shape=(like, like, like, jax.ShapeDtypeStruct((wcols, width), F32)),
        in_specs=[vmem] * 4,
        out_specs=(vmem,) * 4,
        name="keep",
    )(*(pltpu.with_memory_space_constraint(v, pltpu.VMEM) for v in (dq, dk, dv, gp)))
    return dq, dk, dv, gp.T


def solution(mesh):
    spec = P("frame", "space")
    return jax.shard_map(
        local, mesh=mesh, in_specs=(spec,) * 4 + (P("space", "frame"),),
        out_specs=(spec,) * 3 + (P("space", "frame"),), check_vma=False)
```
